256 devices in a mesh: sym: 8 (over x, core), row: 32 (over z, y).
Axes of the slice: x: 4, y: 4, z: 8, core: 2. Of those that a mesh axis runs over, the one named last changes fastest.
Arguments:
- vectors: float32 [8, 131072, 256], P('sym', 'row'), may hold values from -6 to 6
- reflectors: float32 [8, 131072, 512], P('sym', 'row'), may hold values from -0.5 to 0.5
- factors: float32 [8, 4, 128, 128], P('sym'), may hold values from -0.015625 to 0.015625
- tiles: bfloat16 [8, 64, 512, 512], P('sym', 'row'), may hold values from -0.0014648438 to 0.0014648438
- tile_left: int32 [8, 64], P('sym', 'row'), may hold values from 0 to 7
- tile_right: int32 [8, 64], P('sym', 'row'), may hold values from 0 to 7
- tile_occupied_mask: int32 [8, 64], P('sym', 'row'), may hold values 0 or 1
- channels: int32 [8, 256], P('sym', 'row'), may hold values from 256 to 512
Outputs:
- dipole: float32 [8, 256, 256], P('sym', 'row')
The draws below stay inside these ranges and needn't reach their ends.
All inputs are finite; a program needn't handle non-finite values. No bound on the sum of `tile_occupied_mask` on one device may be relied on, other than what follows from the above.
Results may differ from the reference program's by a relative error of at most 0.0049.
Values may be sent and summed in bfloat16 or wider, within the bound.
No kernel may reach another device: no remote copies, remote signals or barrier semaphores. Data moves between devices by JAX's collectives and lax.ppermute only.
A program may use at most 64 MiB of HBM per device.

```python
import jax
import jax.numpy as jnp
from jax import lax

EIG = 256
PANEL = 128
PANELS = 4
BLOCK = 512
TILE_SLOTS = 2
ORDER = 131072
SYMS = 8
BLOCKS_DEV = 8
BLOCKS = 256
TILES = 64


def set_ends(entries, rng, smallest, largest):
    extent = entries.shape
    place = [jax.random.randint(jax.random.fold_in(rng, axis), (), 0, extent[axis]) for axis in range(len(extent))]
    entries = entries.at[tuple(place)].set(smallest)
    longest = extent.index(max(extent))
    place[longest] = (place[longest] + 1) % extent[longest]
    return entries.at[tuple(place)].set(largest)


def levels(own_key, shape, shards, low, high):
    loudness = 1.0
    for dim, blocks in shards:
        heights = jax.random.uniform(jax.random.fold_in(jax.random.fold_in(own_key, 6), dim), (blocks,), jnp.float32, low / len(shards), high / len(shards))
        loudness = loudness * jnp.repeat(jnp.exp(heights), shape[dim] // blocks).reshape((-1,) + (1,) * (len(shape) - 1 - dim))
    return loudness


def bell_draw(rng, extent, scale, reach, cuts=(), held_as=jnp.bfloat16):
    drawn = scale * jax.random.normal(rng, extent, jnp.float32)
    if cuts:
        drawn = drawn * levels(rng, extent, cuts, -0.22, 0.18)
    return jnp.clip(drawn, -reach, reach).astype(held_as)


def setup_inputs(seed: int = 0) -> dict:
    key_of = jax.random.split(jax.random.key(seed), 9)
    vectors = bell_draw(key_of[0], (SYMS, ORDER, EIG), 1.0, 6.0, ((0, 8), (1, 32)), jnp.float32)
    reflectors = bell_draw(key_of[1], (SYMS, ORDER, PANELS * PANEL), PANEL ** -0.5, 0.5, ((0, 8), (1, 32)), jnp.float32)
    factors = bell_draw(key_of[2], (SYMS, PANELS, PANEL, PANEL), ORDER ** -0.5, 0.015625, ((0, 8),), jnp.float32)
    tiles = bell_draw(key_of[3], (SYMS, TILES, BLOCK, BLOCK), (BLOCK * BLOCK * TILES) ** -0.5, 0.0014648438, ((0, 8), (1, 32)))
    tile_left = set_ends(jax.random.randint(key_of[4], (SYMS, TILES), 0, BLOCKS_DEV), jax.random.fold_in(key_of[4], 1), 0, BLOCKS_DEV - 1).astype(jnp.int32)
    tile_right = set_ends(jax.random.randint(key_of[5], (SYMS, TILES), 0, BLOCKS_DEV), jax.random.fold_in(key_of[5], 1), 0, BLOCKS_DEV - 1).astype(jnp.int32)
    tile_occupied_mask = set_ends((jax.random.randint(key_of[6], (SYMS, TILES), 0, 4) < 3).astype(jnp.int32), jax.random.fold_in(key_of[6], 1), 0, 1)
    channels = set_ends(jax.random.randint(key_of[7], (SYMS, BLOCKS), BLOCK // 2, BLOCK + 1), jax.random.fold_in(key_of[7], 1), BLOCK // 2, BLOCK).astype(jnp.int32)
    return {"vectors": vectors, "reflectors": reflectors, "factors": factors, "tiles": tiles, "tile_left": tile_left, "tile_right": tile_right, "tile_occupied_mask": tile_occupied_mask, "channels": channels}


PRECISE = lax.Precision.HIGHEST


def back_transform(start, panels, factor_set):
    result = start
    for level in reversed(range(PANELS)):
        panel = panels[:, level * PANEL:(level + 1) * PANEL]
        inner_part = jnp.dot(panel.T, result, precision=PRECISE)
        result = result - jnp.dot(panel, jnp.dot(factor_set[level], inner_part, precision=PRECISE), precision=PRECISE)
    return result


def reference(vectors, reflectors, factors, tiles, tile_left, tile_right, tile_occupied_mask, channels):
    masked = []
    position = jnp.arange(BLOCK, dtype=jnp.int32)
    for symmetry_label in range(SYMS):
        result = back_transform(vectors[symmetry_label], reflectors[symmetry_label], factors[symmetry_label])
        keeper = (position[None, :] < channels[symmetry_label][:, None]).astype(jnp.float32)
        reshaped_block = result.reshape(BLOCKS, BLOCK, EIG) * keeper[:, :, None]
        masked.append(reshaped_block.astype(jnp.bfloat16))
    offsets = (jnp.arange(TILES, dtype=jnp.int32) // TILE_SLOTS) * BLOCKS_DEV
    dipole_output_list = []
    for symmetry_label in range(SYMS):
        paired_symmetry = (symmetry_label + 1) % SYMS
        bra_state_rows = masked[symmetry_label][(offsets + tile_left[symmetry_label]).astype(jnp.int32)]
        right_rows = masked[paired_symmetry][(offsets + tile_right[symmetry_label]).astype(jnp.int32)]
        bra_ket_product = jnp.einsum("tij,tjk->tik", tiles[symmetry_label].astype(jnp.float32), right_rows.astype(jnp.float32)).astype(jnp.bfloat16)
        tile_presence_mask = tile_occupied_mask[symmetry_label].astype(jnp.float32)
        dipole_output_list.append(jnp.einsum("agx,agh,a->xh", bra_state_rows.astype(jnp.float32), bra_ket_product.astype(jnp.float32), tile_presence_mask))
    return jnp.stack(dipole_output_list)
```

```python
import jax
import jax.numpy as jnp
from jax import lax
from jax.experimental import pallas as pl
from jax.experimental.pallas import tpu as pltpu
from jax.sharding import PartitionSpec as P

F32 = jnp.float32
BF16 = jnp.bfloat16
F16 = jnp.float16
BLOCK = 512
STEP = 512
HALF = 16
PROJ = 2 * HALF
COUP = 24
SHARE = PROJ + COUP + 8
COUPLING_SCALE = 32.0


def split(x):
    high = x.astype(BF16)
    return high, (x - high.astype(F32)).astype(BF16)


def dot(a, b, dims=((1,), (0,))):
    return lax.dot_general(a, b, (dims, ((), ())), preferred_element_type=F32)


def dot3(a, b, dims=((1,), (0,))):
    (ah, al), (bh, bl) = a, b
    return dot(ah, bh, dims) + (dot(ah, bl, dims) + dot(al, bh, dims))


def gram_kernel(start_ref, panel_ref, out_ref, proj, coup, first):
    step = pl.program_id(0)

    @pl.when(step == 0)
    def _():
        proj[...] = jnp.zeros_like(proj)
        coup[...] = jnp.zeros_like(coup)
        first[...] = jnp.zeros_like(first)

    panels = panel_ref[0]
    width = panels.shape[1] // 4
    turned = split(panels.T)
    late = split(panels[:, 2 * width :])
    second = split(panels[:, width : 2 * width])
    start = split(start_ref[0])

    def rows(pair, begin, end):
        return tuple(p[begin:end] for p in pair)

    proj[...] += dot3(turned, start)
    coup[...] += dot3(rows(turned, 0, 3 * width), late)
    first[...] += dot3(rows(turned, 0, width), second)

    @pl.when(step == pl.num_programs(0) - 1)
    def _():
        inner = proj[...]
        top = jnp.max(jnp.abs(inner), axis=(0, 1), keepdims=True)
        exponent = jnp.ceil(jnp.log2(jnp.maximum(top, 1e-30))) - 14.0
        inner = inner * jnp.exp2(-exponent)
        count = out_ref.shape[0]
        out_ref[:, :HALF, :] = inner[:, :128].reshape(count, HALF, 128)
        out_ref[:, HALF:PROJ, :] = inner[:, 128:].reshape(count, HALF, 128)
        lines = jnp.concatenate(
            [
                coup[: 2 * width, :width],
                first[...],
                coup[:, width:],
            ],
            axis=0,
        )
        lines = lines * COUPLING_SCALE
        out_ref[:, PROJ : PROJ + COUP, :] = lines.reshape(count, COUP, 128)
        out_ref[:, PROJ + COUP :, :] = jnp.broadcast_to(
            exponent.reshape(1, 1, 1), (count, 8, 128)
        )


def local_grams(start, panels, count):
    rows, eigen = start.shape[1:]
    columns = panels.shape[2]
    return pl.pallas_call(
        gram_kernel,
        out_shape=jax.ShapeDtypeStruct((count, SHARE, 128), F32),
        grid=(rows // STEP,),
        in_specs=[
            pl.BlockSpec((1, STEP, eigen), lambda i: (0, i, 0)),
            pl.BlockSpec((1, STEP, columns), lambda i: (0, i, 0)),
        ],
        out_specs=pl.BlockSpec((count, SHARE, 128), lambda i: (0, 0, 0)),
        scratch_shapes=[
            pltpu.VMEM((columns, eigen), F32),
            pltpu.VMEM((3 * columns // 4, columns // 2), F32),
            pltpu.VMEM((columns // 4, columns // 4), F32),
        ],
        compiler_params=pltpu.CompilerParams(vmem_limit_bytes=40 << 20),
        cost_estimate=pl.CostEstimate(
            flops=6 * rows * columns * (eigen + columns // 2),
            bytes_accessed=4 * rows * (eigen + columns),
            transcendentals=0,
        ),
        name="grams",
    )(start, panels)


def updated_block(start_ref, panel_ref, upper, lower, limit):
    high, low = split(panel_ref[0])
    back = start_ref[0] - (
        dot(high, upper[...]) + (dot(high, lower[...]) + dot(low, upper[...]))
    )
    line = lax.broadcasted_iota(jnp.int32, back.shape, 0)
    return jnp.where(line < limit, back, 0.0).astype(BF16)


def solve_kernel(
    want_ref, limit_ref, sums_ref, factor_ref, start_ref, panel_ref, out_ref, upper, lower
):
    turn = pl.program_id(0)
    count = sums_ref.shape[0]
    width = factor_ref.shape[2]

    @pl.when(turn == 0)
    def _():
        scale = jnp.exp2(sums_ref[:, PROJ + COUP : PROJ + COUP + 1, :])
        size = (count * HALF, 128)
        inner = jnp.concatenate(
            [
                (sums_ref[:, :HALF, :] * scale).reshape(size),
                (sums_ref[:, HALF:PROJ, :] * scale).reshape(size),
            ],
            axis=1,
        )
        links = split(sums_ref[:, PROJ : PROJ + COUP, :].reshape(count * COUP, 128))

        def link(begin, end):
            return tuple(p[begin * width : end * width] for p in links)

        current = [inner[k * width : (k + 1) * width] for k in range(4)]
        parts = [None] * 4
        reach = {3: (3, 6), 2: (0, 2), 1: (2, 3)}
        for level in (3, 2, 1, 0):
            update = split(dot3(split(factor_ref[0, level]), split(current[level])))
            parts[level] = update
            if level:
                moved = dot3(link(*reach[level]), update)
                for k in range(level):
                    current[k] = current[k] - moved[k * width : (k + 1) * width]
        upper[...] = jnp.concatenate([p[0] for p in parts], axis=0)
        lower[...] = jnp.concatenate([p[1] for p in parts], axis=0)

    out_ref[0] = updated_block(
        start_ref, panel_ref, upper, lower, limit_ref[want_ref[turn]]
    )


def left_kernel(
    left_ref, occupied_ref, limit_ref, upper, lower, start_ref, panel_ref, out_ref
):
    turn = pl.program_id(0)
    limit = limit_ref[left_ref[turn]] * occupied_ref[turn]
    out_ref[0] = updated_block(start_ref, panel_ref, upper, lower, limit)


def blocks_of(width):
    return pl.BlockSpec((1, BLOCK, width), lambda t, which, *_: (0, which[t], 0))


def whole(shape):
    return pl.BlockSpec(shape, lambda t, *_: (0,) * len(shape))


def solve_and_update(want, limits, sums, factors, start, panels):
    count = want.shape[0]
    eigen, columns = start.shape[2], panels.shape[2]
    coefficients = jax.ShapeDtypeStruct((columns, eigen), BF16)
    return pl.pallas_call(
        solve_kernel,
        out_shape=(
            jax.ShapeDtypeStruct((count, BLOCK, eigen), BF16),
            coefficients,
            coefficients,
        ),
        grid_spec=pltpu.PrefetchScalarGridSpec(
            num_scalar_prefetch=2,
            grid=(count,),
            in_specs=[
                whole(sums.shape),
                whole(factors.shape),
                blocks_of(eigen),
                blocks_of(columns),
            ],
            out_specs=(
                pl.BlockSpec((1, BLOCK, eigen), lambda t, *_: (t, 0, 0)),
                whole((columns, eigen)),
                whole((columns, eigen)),
            ),
        ),
        compiler_params=pltpu.CompilerParams(vmem_limit_bytes=32 << 20),
        cost_estimate=pl.CostEstimate(
            flops=6 * count * BLOCK * columns * eigen,
            bytes_accessed=4 * count * BLOCK * (columns + eigen),
            transcendentals=0,
        ),
        name="solve",
    )(want, limits, sums, factors, start, panels)


def left_blocks(left, occupied, limits, upper, lower, start, panels):
    count = left.shape[0]
    eigen, columns = start.shape[2], panels.shape[2]
    return pl.pallas_call(
        left_kernel,
        out_shape=jax.ShapeDtypeStruct((count, BLOCK, eigen), BF16),
        grid_spec=pltpu.PrefetchScalarGridSpec(
            num_scalar_prefetch=3,
            grid=(count,),
            in_specs=[
                whole((columns, eigen)),
                whole((columns, eigen)),
                blocks_of(eigen),
                blocks_of(columns),
            ],
            out_specs=pl.BlockSpec((1, BLOCK, eigen), lambda t, *_: (t, 0, 0)),
        ),
        compiler_params=pltpu.CompilerParams(vmem_limit_bytes=32 << 20),
        cost_estimate=pl.CostEstimate(
            flops=6 * count * BLOCK * columns * eigen,
            bytes_accessed=4 * count * BLOCK * (columns + eigen),
            transcendentals=0,
        ),
        name="left",
    )(left, occupied, limits, upper, lower, start, panels)


def dipole_kernel(tile_ref, right_ref, left_ref, out_ref):
    total = None
    for t in range(tile_ref.shape[1]):
        product = dot(tile_ref[0, t], right_ref[t]).astype(BF16)
        term = dot(left_ref[t], product, ((0,), (0,)))
        total = term if total is None else total + term
    out_ref[...] = total.astype(BF16)


def tile_products(tiles, right, left):
    eigen = right.shape[2]
    return pl.pallas_call(
        dipole_kernel,
        out_shape=jax.ShapeDtypeStruct((eigen, eigen), BF16),
        compiler_params=pltpu.CompilerParams(vmem_limit_bytes=32 << 20),
        name="dipole",
    )(tiles, right, left)


def passed_along(block, axis, distance):
    devices = range(lax.axis_size(axis))
    route = [((i - distance) % len(devices), i) for i in devices]
    return lax.ppermute(block, axis, route)


def exchanged(shares):
    return lax.all_to_all(shares, "row", 0, 0, tiled=True)


def on_device(
    vectors, reflectors, factors, tiles, tile_left, tile_right, tile_occupied_mask, channels
):
    count = lax.axis_size("row")
    vectors = pltpu.with_memory_space_constraint(vectors, pltpu.HBM)
    reflectors = pltpu.with_memory_space_constraint(reflectors, pltpu.HBM)
    want = passed_along(tile_right[0], "sym", 1)
    shares = local_grams(vectors, reflectors, count)
    terms = exchanged(shares.astype(F16)).astype(F32)
    exponents = terms[:, PROJ + COUP :]
    proj = jnp.sum(terms[:, :PROJ] * jnp.exp2(exponents[:, :1]), axis=0)
    coup = jnp.sum(terms[:, PROJ : PROJ + COUP], axis=0) * (1.0 / COUPLING_SCALE)
    exponent = jnp.max(exponents, axis=0) + 5.0
    owned = jnp.concatenate([proj * jnp.exp2(-exponent[:1]), coup, exponent], axis=0)
    copies = jnp.broadcast_to(owned.astype(F16), (count, SHARE, 128))
    sums = exchanged(copies).astype(F32)
    packed, upper, lower = solve_and_update(
        want, channels[0], sums, factors, vectors, reflectors
    )
    right = passed_along(packed, "sym", -1)
    left = left_blocks(
        tile_left[0], tile_occupied_mask[0], channels[0], upper, lower, vectors, reflectors
    )
    partial = tile_products(tiles, right, left)
    eigen = partial.shape[1]
    owned = exchanged(partial.reshape(count, eigen // count, eigen))
    return jnp.sum(owned.astype(F32), axis=0)[None]


def solution(mesh):
    return jax.shard_map(
        on_device,
        mesh=mesh,
        in_specs=(
            P("sym", "row", None),
            P("sym", "row", None),
            P("sym", None, None, None),
            P("sym", "row", None, None),
            P("sym", "row"),
            P("sym", "row"),
            P("sym", "row"),
            P("sym", "row"),
        ),
        out_specs=P("sym", "row", None),
        check_vma=False,
    )
```

```python
import jax
import jax.numpy as jnp
from jax import lax
from jax.experimental import pallas as pl
from jax.experimental.pallas import tpu as pltpu
from jax.sharding import PartitionSpec as P

F32 = jnp.float32
BF16 = jnp.bfloat16
F16 = jnp.float16
BLOCK = 512
STEP = 1024
HALF = 16
PROJ = 2 * HALF
COUP = 24
SHARE = PROJ + COUP + 8
COUPLING_SCALE = 32.0


ROWS = ((0,), (0,))


def split(x):
    high = x.astype(BF16)
    return high, (x - high.astype(F32)).astype(BF16)


def dot(a, b, dims=((1,), (0,))):
    return lax.dot_general(a, b, (dims, ((), ())), preferred_element_type=F32)


def dot3(a, b, dims=((1,), (0,))):
    (ah, al), (bh, bl) = a, b
    return dot(ah, bh, dims) + (dot(ah, bl, dims) + dot(al, bh, dims))


def gram_kernel(start_ref, panel_ref, out_ref, proj, coup, first):
    step = pl.program_id(0)

    @pl.when(step == 0)
    def _():
        proj[...] = jnp.zeros_like(proj)
        coup[...] = jnp.zeros_like(coup)
        first[...] = jnp.zeros_like(first)

    panels = split(panel_ref[0])
    start = split(start_ref[0])
    width = panel_ref.shape[2] // 4

    def columns(begin, end):
        return tuple(p[:, begin * width : end * width] for p in panels)

    proj[...] += dot3(panels, start, ROWS)
    coup[...] += dot3(columns(0, 3), columns(2, 4), ROWS)
    first[...] += dot3(columns(0, 1), columns(1, 2), ROWS)

    @pl.when(step == pl.num_programs(0) - 1)
    def _():
        inner = proj[...]
        top = jnp.max(jnp.abs(inner), axis=(0, 1), keepdims=True)
        exponent = jnp.ceil(jnp.log2(jnp.maximum(top, 1e-30))) - 14.0
        inner = inner * jnp.exp2(-exponent)
        count = out_ref.shape[0]
        out_ref[:, :HALF, :] = inner[:, :128].reshape(count, HALF, 128)
        out_ref[:, HALF:PROJ, :] = inner[:, 128:].reshape(count, HALF, 128)
        lines = jnp.concatenate(
            [
                coup[: 2 * width, :width],
                first[...],
                coup[:, width:],
            ],
            axis=0,
        )
        lines = lines * COUPLING_SCALE
        out_ref[:, PROJ : PROJ + COUP, :] = lines.reshape(count, COUP, 128)
        out_ref[:, PROJ + COUP :, :] = jnp.broadcast_to(
            exponent.reshape(1, 1, 1), (count, 8, 128)
        )


def local_grams(start, panels, count):
    rows, eigen = start.shape[1:]
    columns = panels.shape[2]
    return pl.pallas_call(
        gram_kernel,
        out_shape=jax.ShapeDtypeStruct((count, SHARE, 128), F32),
        grid=(rows // STEP,),
        in_specs=[
            pl.BlockSpec((1, STEP, eigen), lambda i: (0, i, 0)),
            pl.BlockSpec((1, STEP, columns), lambda i: (0, i, 0)),
        ],
        out_specs=pl.BlockSpec((count, SHARE, 128), lambda i: (0, 0, 0)),
        scratch_shapes=[
            pltpu.VMEM((columns, eigen), F32),
            pltpu.VMEM((3 * columns // 4, columns // 2), F32),
            pltpu.VMEM((columns // 4, columns // 4), F32),
        ],
        compiler_params=pltpu.CompilerParams(vmem_limit_bytes=40 << 20),
        cost_estimate=pl.CostEstimate(
            flops=6 * rows * columns * (eigen + columns // 2),
            bytes_accessed=4 * rows * (eigen + columns),
            transcendentals=0,
        ),
        name="grams",
    )(start, panels)


def updated_block(start, panels, upper, lower, limit):
    high, low = split(panels)
    back = start - (dot(high, upper) + (dot(high, lower) + dot(low, upper)))
    line = lax.broadcasted_iota(jnp.int32, back.shape, 0)
    return jnp.where(line < limit, back, 0.0).astype(BF16)


def solve_kernel(
    want_ref,
    limit_ref,
    sums_ref,
    factor_ref,
    start_ref,
    panel_ref,
    out_ref,
    upper,
    lower,
    starts,
    panels,
    arrived,
):
    copies = []
    for t in range(out_ref.shape[0]):
        rows = pl.ds(pl.multiple_of(want_ref[t] * BLOCK, BLOCK), BLOCK)
        for source, target, kind in ((panel_ref, panels, 0), (start_ref, starts, 1)):
            copy = pltpu.make_async_copy(
                source.at[0, rows], target.at[t], arrived.at[kind, t]
            )
            copy.start()
            copies.append(copy)
    count = sums_ref.shape[0]
    width = factor_ref.shape[2]
    scale = jnp.exp2(sums_ref[:, PROJ + COUP : PROJ + COUP + 1, :])
    size = (count * HALF, 128)
    inner = split(
        jnp.concatenate(
            [
                (sums_ref[:, :HALF, :] * scale).reshape(size),
                (sums_ref[:, HALF:PROJ, :] * scale).reshape(size),
            ],
            axis=1,
        )
    )
    links = split(sums_ref[:, PROJ : PROJ + COUP, :].reshape(count * COUP, 128))

    def part(pair, k):
        return tuple(p[k * width : (k + 1) * width] for p in pair)

    factors = [split(factor_ref[0, level]) for level in range(4)]
    current = [dot3(factors[level], part(inner, level)) for level in range(4)]
    places = {3: ((0, 3), (1, 4), (2, 5)), 2: ((0, 0), (1, 1)), 1: ((0, 2),)}
    chained = {}
    for later, pairs in places.items():
        chained[later] = split(
            jnp.concatenate([dot3(factors[k], part(links, at)) for k, at in pairs], axis=0)
        )
    parts = [None] * 4
    for level in (3, 2, 1, 0):
        parts[level] = split(current[level])
        if level:
            moved = dot3(chained[level], parts[level])
            for k in range(level):
                current[k] = current[k] - moved[k * width : (k + 1) * width]
    upper[...] = jnp.concatenate([p[0] for p in parts], axis=0)
    lower[...] = jnp.concatenate([p[1] for p in parts], axis=0)
    for t in range(out_ref.shape[0]):
        copies[2 * t].wait()
        copies[2 * t + 1].wait()
        out_ref[t] = updated_block(
            starts[t], panels[t], upper[...], lower[...], limit_ref[want_ref[t]]
        )


def left_kernel(
    left_ref, occupied_ref, limit_ref, upper, lower, start_ref, panel_ref, out_ref
):
    turn = pl.program_id(0)
    out_ref[0] = updated_block(
        start_ref[0],
        panel_ref[0],
        upper[...],
        lower[...],
        limit_ref[left_ref[turn]] * occupied_ref[turn],
    )


SCALARS = pl.BlockSpec(memory_space=pltpu.SMEM)
ARRAY = pl.BlockSpec(memory_space=pltpu.VMEM)
FAR = pl.BlockSpec(memory_space=pltpu.HBM)


def update_cost(blocks, columns, eigen):
    return pl.CostEstimate(
        flops=6 * blocks * BLOCK * columns * eigen,
        bytes_accessed=4 * blocks * BLOCK * (columns + eigen),
        transcendentals=0,
    )


def solve_and_update(want, limits, sums, factors, start, panels):
    count = want.shape[0]
    eigen, columns = start.shape[2], panels.shape[2]
    coefficients = jax.ShapeDtypeStruct((columns, eigen), BF16)
    return pl.pallas_call(
        solve_kernel,
        out_shape=(
            jax.ShapeDtypeStruct((count, BLOCK, eigen), BF16),
            coefficients,
            coefficients,
        ),
        in_specs=[SCALARS, SCALARS, ARRAY, ARRAY, FAR, FAR],
        out_specs=(ARRAY,) * 3,
        scratch_shapes=[
            pltpu.VMEM((count, BLOCK, eigen), F32),
            pltpu.VMEM((count, BLOCK, columns), F32),
            pltpu.SemaphoreType.DMA((2, count)),
        ],
        compiler_params=pltpu.CompilerParams(vmem_limit_bytes=16 << 20),
        cost_estimate=update_cost(count, columns, eigen),
        name="solve",
    )(want, limits, sums, factors, start, panels)


def left_blocks(left, occupied, limits, upper, lower, start, panels):
    count = left.shape[0]
    eigen, columns = start.shape[2], panels.shape[2]

    def named(width):
        return pl.BlockSpec((1, BLOCK, width), lambda t, which, *_: (0, which[t], 0))

    def whole(shape):
        return pl.BlockSpec(shape, lambda t, *_: (0, 0))

    return pl.pallas_call(
        left_kernel,
        out_shape=jax.ShapeDtypeStruct((count, BLOCK, eigen), BF16),
        grid_spec=pltpu.PrefetchScalarGridSpec(
            num_scalar_prefetch=3,
            grid=(count,),
            in_specs=[
                whole((columns, eigen)),
                whole((columns, eigen)),
                named(eigen),
                named(columns),
            ],
            out_specs=pl.BlockSpec((1, BLOCK, eigen), lambda t, *_: (t, 0, 0)),
        ),
        compiler_params=pltpu.CompilerParams(vmem_limit_bytes=16 << 20),
        cost_estimate=update_cost(count, columns, eigen),
        name="left",
    )(left, occupied, limits, upper, lower, start, panels)


def dipole_kernel(tile_ref, right_ref, left_ref, out_ref):
    total = None
    for t in range(tile_ref.shape[1]):
        product = dot(tile_ref[0, t], right_ref[t]).astype(BF16)
        term = dot(left_ref[t], product, ((0,), (0,)))
        total = term if total is None else total + term
    out_ref[...] = total.astype(BF16)


def tile_products(tiles, right, left):
    eigen = right.shape[2]
    return pl.pallas_call(
        dipole_kernel,
        out_shape=jax.ShapeDtypeStruct((eigen, eigen), BF16),
        compiler_params=pltpu.CompilerParams(vmem_limit_bytes=8 << 20),
        name="dipole",
    )(tiles, right, left)


def passed_along(block, axis, distance):
    devices = range(lax.axis_size(axis))
    route = [((i - distance) % len(devices), i) for i in devices]
    return lax.ppermute(block, axis, route)


def exchanged(shares):
    return lax.all_to_all(shares, "row", 0, 0, tiled=True)


def on_device(
    vectors, reflectors, factors, tiles, tile_left, tile_right, tile_occupied_mask, channels
):
    count = lax.axis_size("row")
    vectors = pltpu.with_memory_space_constraint(vectors, pltpu.HBM)
    reflectors = pltpu.with_memory_space_constraint(reflectors, pltpu.HBM)
    want = passed_along(tile_right[0], "sym", 1)
    shares = local_grams(vectors, reflectors, count).astype(F16)
    want, shares = lax.optimization_barrier((want, shares))
    terms = exchanged(shares).astype(F32)
    exponents = terms[:, PROJ + COUP :]
    proj = jnp.sum(terms[:, :PROJ] * jnp.exp2(exponents[:, :1]), axis=0)
    coup = jnp.sum(terms[:, PROJ : PROJ + COUP], axis=0) * (1.0 / COUPLING_SCALE)
    exponent = jnp.max(exponents, axis=0) + 5.0
    owned = jnp.concatenate([proj * jnp.exp2(-exponent[:1]), coup, exponent], axis=0)
    copies = jnp.broadcast_to(owned.astype(F16), (count, SHARE, 128))
    sums = exchanged(copies).astype(F32)
    packed, upper, lower = solve_and_update(
        want, channels[0], sums, factors, vectors, reflectors
    )
    right = passed_along(packed, "sym", -1)
    left = left_blocks(
        tile_left[0], tile_occupied_mask[0], channels[0], upper, lower, vectors, reflectors
    )
    partial = tile_products(tiles, right, left)
    eigen = partial.shape[1]
    owned = exchanged(partial.reshape(count, eigen // count, eigen))
    return jnp.sum(owned.astype(F32), axis=0)[None]


def solution(mesh):
    return jax.shard_map(
        on_device,
        mesh=mesh,
        in_specs=(
            P("sym", "row", None),
            P("sym", "row", None),
            P("sym", None, None, None),
            P("sym", "row", None, None),
            P("sym", "row"),
            P("sym", "row"),
            P("sym", "row"),
            P("sym", "row"),
        ),
        out_specs=P("sym", "row", None),
        check_vma=False,
    )
```

```python
import jax
import jax.numpy as jnp
from jax import lax
from jax.experimental import pallas as pl
from jax.experimental.pallas import tpu as pltpu
from jax.sharding import PartitionSpec as P

F32 = jnp.float32
BF16 = jnp.bfloat16
F16 = jnp.float16
BLOCK = 512
STEP = 1024
NEAR = 8
HALF = 64
PROJ = 2 * HALF
COUP = 96
BODY = PROJ + COUP
SHARE = BODY + 8
COUPLING_SCALE = 32.0
ROWS = ((0,), (0,))


def split(x):
    high = x.astype(BF16)
    return high, (x - high.astype(F32)).astype(BF16)


def dot(a, b, dims=((1,), (0,))):
    return lax.dot_general(a, b, (dims, ((), ())), preferred_element_type=F32)


def dot3(a, b, dims=((1,), (0,))):
    (ah, al), (bh, bl) = a, b
    return dot(ah, bh, dims) + (dot(ah, bl, dims) + dot(al, bh, dims))


def gram_kernel(start_ref, panel_ref, out_ref, proj, coup, first):
    step = pl.program_id(0)

    @pl.when(step == 0)
    def _():
        proj[...] = jnp.zeros_like(proj)
        coup[...] = jnp.zeros_like(coup)
        first[...] = jnp.zeros_like(first)

    panels = split(panel_ref[0])
    start = split(start_ref[0])
    width = panel_ref.shape[2] // 4

    def columns(begin, end):
        return tuple(p[:, begin * width : end * width] for p in panels)

    proj[...] += dot3(panels, start, ROWS)
    coup[...] += dot3(columns(0, 3), columns(2, 4), ROWS)
    first[...] += dot3(columns(0, 1), columns(1, 2), ROWS)

    @pl.when(step == pl.num_programs(0) - 1)
    def _():
        inner = proj[...]
        top = jnp.max(jnp.abs(inner), axis=(0, 1), keepdims=True)
        exponent = jnp.ceil(jnp.log2(jnp.maximum(top, 1e-30))) - 14.0
        inner = inner * jnp.exp2(-exponent)
        count = out_ref.shape[0]
        out_ref[:, :HALF, :] = inner[:, :128].reshape(count, HALF, 128)
        out_ref[:, HALF:PROJ, :] = inner[:, 128:].reshape(count, HALF, 128)
        lines = jnp.concatenate(
            [
                coup[: 2 * width, :width],
                first[...],
                coup[:, width:],
            ],
            axis=0,
        )
        lines = lines * COUPLING_SCALE
        out_ref[:, PROJ:BODY, :] = lines.reshape(count, COUP, 128)
        out_ref[:, BODY:, :] = jnp.broadcast_to(
            exponent.reshape(1, 1, 1), (count, 8, 128)
        )


def local_grams(start, panels, count):
    rows, eigen = start.shape[1:]
    columns = panels.shape[2]
    return pl.pallas_call(
        gram_kernel,
        out_shape=jax.ShapeDtypeStruct((count, SHARE, 128), F32),
        grid=(rows // STEP,),
        in_specs=[
            pl.BlockSpec((1, STEP, eigen), lambda i: (0, i, 0)),
            pl.BlockSpec((1, STEP, columns), lambda i: (0, i, 0)),
        ],
        out_specs=pl.BlockSpec((count, SHARE, 128), lambda i: (0, 0, 0)),
        scratch_shapes=[
            pltpu.VMEM((columns, eigen), F32),
            pltpu.VMEM((3 * columns // 4, columns // 2), F32),
            pltpu.VMEM((columns // 4, columns // 4), F32),
        ],
        compiler_params=pltpu.CompilerParams(vmem_limit_bytes=40 << 20),
        cost_estimate=pl.CostEstimate(
            flops=6 * rows * columns * (eigen + columns // 2),
            bytes_accessed=4 * rows * (eigen + columns),
            transcendentals=0,
        ),
        name="grams",
    )(start, panels)


def updated_block(start, panels, upper, lower, limit):
    high, low = panels
    back = start - (dot(high, upper) + (dot(high, lower) + dot(low, upper)))
    line = lax.broadcasted_iota(jnp.int32, back.shape, 0)
    return jnp.where(line < limit, back, 0.0).astype(BF16)


def solve_kernel(
    want_ref,
    limit_ref,
    sums_ref,
    exponent_ref,
    factor_ref,
    start_ref,
    panel_ref,
    out_ref,
    upper,
    lower,
    starts,
    panels,
    arrived,
):
    copies = []
    for t in range(out_ref.shape[0]):
        rows = pl.ds(pl.multiple_of(want_ref[t] * BLOCK, BLOCK), BLOCK)
        for source, target, kind in ((panel_ref, panels, 0), (start_ref, starts, 1)):
            copy = pltpu.make_async_copy(
                source.at[0, rows], target.at[t], arrived.at[kind, t]
            )
            copy.start()
            copies.append(copy)
    count = sums_ref.shape[0]
    width = factor_ref.shape[2]
    scale = jnp.exp2(exponent_ref[:1, :])
    size = (count * HALF, 128)
    inner = split(
        jnp.concatenate(
            [
                sums_ref[:, :HALF, :].reshape(size) * scale,
                sums_ref[:, HALF:PROJ, :].reshape(size) * scale,
            ],
            axis=1,
        )
    )
    links = split(sums_ref[:, PROJ:BODY, :].reshape(count * COUP, 128))

    def part(pair, k):
        return tuple(p[k * width : (k + 1) * width] for p in pair)

    factors = [split(factor_ref[0, level]) for level in range(4)]
    current = [dot3(factors[level], part(inner, level)) for level in range(4)]
    places = {3: ((0, 3), (1, 4), (2, 5)), 2: ((0, 0), (1, 1)), 1: ((0, 2),)}
    chained = {}
    for later, pairs in places.items():
        chained[later] = split(
            jnp.concatenate([dot3(factors[k], part(links, at)) for k, at in pairs], axis=0)
        )
    for copy in copies:
        copy.wait()
    fetched = [split(panels[t]) for t in range(out_ref.shape[0])]
    parts = [None] * 4
    for level in (3, 2, 1, 0):
        parts[level] = split(current[level])
        if level:
            moved = dot3(chained[level], parts[level])
            for k in range(level):
                current[k] = current[k] - moved[k * width : (k + 1) * width]
    upper[...] = jnp.concatenate([p[0] for p in parts], axis=0)
    lower[...] = jnp.concatenate([p[1] for p in parts], axis=0)
    for t in range(out_ref.shape[0]):
        out_ref[t] = updated_block(
            starts[t], fetched[t], upper[...], lower[...], limit_ref[want_ref[t]]
        )


def left_kernel(
    left_ref, occupied_ref, limit_ref, upper, lower, start_ref, panel_ref, out_ref
):
    turn = pl.program_id(0)
    out_ref[0] = updated_block(
        start_ref[0],
        split(panel_ref[0]),
        upper[...],
        lower[...],
        limit_ref[left_ref[turn]] * occupied_ref[turn],
    )


SCALARS = pl.BlockSpec(memory_space=pltpu.SMEM)
ARRAY = pl.BlockSpec(memory_space=pltpu.VMEM)
FAR = pl.BlockSpec(memory_space=pltpu.HBM)


def update_cost(blocks, columns, eigen):
    return pl.CostEstimate(
        flops=6 * blocks * BLOCK * columns * eigen,
        bytes_accessed=4 * blocks * BLOCK * (columns + eigen),
        transcendentals=0,
    )


def solve_and_update(want, limits, sums, exponent, factors, start, panels):
    count = want.shape[0]
    eigen, columns = start.shape[2], panels.shape[2]
    coefficients = jax.ShapeDtypeStruct((columns, eigen), BF16)
    return pl.pallas_call(
        solve_kernel,
        out_shape=(
            jax.ShapeDtypeStruct((count, BLOCK, eigen), BF16),
            coefficients,
            coefficients,
        ),
        in_specs=[SCALARS, SCALARS, ARRAY, ARRAY, ARRAY, FAR, FAR],
        out_specs=(ARRAY,) * 3,
        scratch_shapes=[
            pltpu.VMEM((count, BLOCK, eigen), F32),
            pltpu.VMEM((count, BLOCK, columns), F32),
            pltpu.SemaphoreType.DMA((2, count)),
        ],
        compiler_params=pltpu.CompilerParams(vmem_limit_bytes=16 << 20),
        cost_estimate=update_cost(count, columns, eigen),
        name="solve",
    )(want, limits, sums, exponent, factors, start, panels)


def left_blocks(left, occupied, limits, upper, lower, start, panels):
    count = left.shape[0]
    eigen, columns = start.shape[2], panels.shape[2]

    def named(width):
        return pl.BlockSpec((1, BLOCK, width), lambda t, which, *_: (0, which[t], 0))

    def whole(shape):
        return pl.BlockSpec(shape, lambda t, *_: (0, 0))

    return pl.pallas_call(
        left_kernel,
        out_shape=jax.ShapeDtypeStruct((count, BLOCK, eigen), BF16),
        grid_spec=pltpu.PrefetchScalarGridSpec(
            num_scalar_prefetch=3,
            grid=(count,),
            in_specs=[
                whole((columns, eigen)),
                whole((columns, eigen)),
                named(eigen),
                named(columns),
            ],
            out_specs=pl.BlockSpec((1, BLOCK, eigen), lambda t, *_: (t, 0, 0)),
        ),
        compiler_params=pltpu.CompilerParams(vmem_limit_bytes=16 << 20),
        cost_estimate=update_cost(count, columns, eigen),
        name="left",
    )(left, occupied, limits, upper, lower, start, panels)


def dipole_kernel(tile_ref, right_ref, left_ref, out_ref):
    total = None
    for t in range(tile_ref.shape[1]):
        product = dot(tile_ref[0, t], right_ref[t]).astype(BF16)
        term = dot(left_ref[t], product, ((0,), (0,)))
        total = term if total is None else total + term
    out_ref[...] = total.astype(BF16)


def tile_products(tiles, right, left):
    eigen = right.shape[2]
    return pl.pallas_call(
        dipole_kernel,
        out_shape=jax.ShapeDtypeStruct((eigen, eigen), BF16),
        compiler_params=pltpu.CompilerParams(vmem_limit_bytes=8 << 20),
        name="dipole",
    )(tiles, right, left)


def passed_along(block, axis, distance):
    devices = range(lax.axis_size(axis))
    route = [((i - distance) % len(devices), i) for i in devices]
    return lax.ppermute(block, axis, route)


def exchanged(shares, groups=None):
    return lax.all_to_all(shares, "row", 0, 0, axis_index_groups=groups, tiled=True)


def combined(terms):
    count = terms.shape[0]
    terms = terms.astype(F32)
    exponents = terms[:, BODY:]
    proj = jnp.sum(terms[:, :PROJ] * jnp.exp2(exponents[:, :1]), axis=0)
    coup = jnp.sum(terms[:, PROJ:BODY], axis=0) * (1.0 / count)
    exponent = jnp.max(exponents, axis=0) + float(count.bit_length() - 1)
    return proj * jnp.exp2(-exponent[:1]), coup, exponent


def copies_of(parts, count):
    lines = jnp.concatenate(parts, axis=0).astype(F16)
    return jnp.broadcast_to(lines, (count, *lines.shape))


def on_device(
    vectors, reflectors, factors, tiles, tile_left, tile_right, tile_occupied_mask, channels
):
    count = lax.axis_size("row")
    vectors = pltpu.with_memory_space_constraint(vectors, pltpu.HBM)
    reflectors = pltpu.with_memory_space_constraint(reflectors, pltpu.HBM)
    want = passed_along(tile_right[0], "sym", 1)
    far = count // NEAR
    inside = [[far_at * NEAR + at for at in range(NEAR)] for far_at in range(far)]
    across = [[far_at * NEAR + at for far_at in range(far)] for at in range(NEAR)]
    shares = local_grams(vectors, reflectors, NEAR).astype(F16)
    want, shares = lax.optimization_barrier((want, shares))
    owned = combined(exchanged(shares, inside))
    proj, coup, exponent = combined(exchanged(copies_of(owned, far), across))
    sums = exchanged(copies_of((proj, coup), NEAR), inside).astype(F32)
    packed, upper, lower = solve_and_update(
        want, channels[0], sums, exponent, factors, vectors, reflectors
    )
    right = passed_along(packed, "sym", -1)
    left = left_blocks(
        tile_left[0], tile_occupied_mask[0], channels[0], upper, lower, vectors, reflectors
    )
    partial = tile_products(tiles, right, left)
    eigen = partial.shape[1]
    owned = exchanged(partial.reshape(count, eigen // count, eigen))
    return jnp.sum(owned.astype(F32), axis=0)[None]


def solution(mesh):
    return jax.shard_map(
        on_device,
        mesh=mesh,
        in_specs=(
            P("sym", "row", None),
            P("sym", "row", None),
            P("sym", None, None, None),
            P("sym", "row", None, None),
            P("sym", "row"),
            P("sym", "row"),
            P("sym", "row"),
            P("sym", "row"),
        ),
        out_specs=P("sym", "row", None),
        check_vma=False,
    )
```

```python
import functools

import jax
import jax.numpy as jnp
from jax import lax
from jax.experimental import pallas as pl
from jax.experimental.pallas import tpu as pltpu
from jax.sharding import PartitionSpec as P

F32 = jnp.float32
BF16 = jnp.bfloat16
F16 = jnp.float16
BLOCK = 512
STEP = 1024
NEAR = 8
HALF = 64
PROJ = 2 * HALF
COUP = 96
BODY = PROJ + COUP
SHARE = BODY + 8
COUPLING_SCALE = 32.0
ROWS = ((0,), (0,))


def split(x):
    high = x.astype(BF16)
    return high, (x - high.astype(F32)).astype(BF16)


def dot(a, b, dims=((1,), (0,))):
    return lax.dot_general(a, b, (dims, ((), ())), preferred_element_type=F32)


def dot3(a, b, dims=((1,), (0,))):
    (ah, al), (bh, bl) = a, b
    return dot(ah, bh, dims) + (dot(ah, bl, dims) + dot(al, bh, dims))


def gram_kernel(start_ref, panel_ref, out_ref, proj, coup, first):
    step = pl.program_id(0)

    @pl.when(step == 0)
    def _():
        proj[...] = jnp.zeros_like(proj)
        coup[...] = jnp.zeros_like(coup)
        first[...] = jnp.zeros_like(first)

    panels = split(panel_ref[0])
    start = split(start_ref[0])
    width = panel_ref.shape[2] // 4

    def columns(begin, end):
        return tuple(p[:, begin * width : end * width] for p in panels)

    proj[...] += dot3(panels, start, ROWS)
    coup[...] += dot3(columns(0, 3), columns(2, 4), ROWS)
    first[...] += dot3(columns(0, 1), columns(1, 2), ROWS)

    @pl.when(step == pl.num_programs(0) - 1)
    def _():
        inner = proj[...]
        top = jnp.max(jnp.abs(inner), axis=(0, 1), keepdims=True)
        exponent = jnp.ceil(jnp.log2(jnp.maximum(top, 1e-30))) - 14.0
        inner = inner * jnp.exp2(-exponent)
        count = out_ref.shape[0]
        out_ref[:, :HALF, :] = inner[:, :128].reshape(count, HALF, 128)
        out_ref[:, HALF:PROJ, :] = inner[:, 128:].reshape(count, HALF, 128)
        lines = jnp.concatenate(
            [
                coup[: 2 * width, :width],
                first[...],
                coup[:, width:],
            ],
            axis=0,
        )
        lines = lines * COUPLING_SCALE
        out_ref[:, PROJ:BODY, :] = lines.reshape(count, COUP, 128)
        out_ref[:, BODY:, :] = jnp.broadcast_to(
            exponent.reshape(1, 1, 1), (count, 8, 128)
        )


def local_grams(start, panels, count):
    rows, eigen = start.shape[1:]
    columns = panels.shape[2]
    return pl.pallas_call(
        gram_kernel,
        out_shape=jax.ShapeDtypeStruct((count, SHARE, 128), F32),
        grid=(rows // STEP,),
        in_specs=[
            pl.BlockSpec((1, STEP, eigen), lambda i: (0, i, 0)),
            pl.BlockSpec((1, STEP, columns), lambda i: (0, i, 0)),
        ],
        out_specs=pl.BlockSpec((count, SHARE, 128), lambda i: (0, 0, 0)),
        scratch_shapes=[
            pltpu.VMEM((columns, eigen), F32),
            pltpu.VMEM((3 * columns // 4, columns // 2), F32),
            pltpu.VMEM((columns // 4, columns // 4), F32),
        ],
        compiler_params=pltpu.CompilerParams(vmem_limit_bytes=40 << 20),
        cost_estimate=pl.CostEstimate(
            flops=6 * rows * columns * (eigen + columns // 2),
            bytes_accessed=4 * rows * (eigen + columns),
            transcendentals=0,
        ),
        name="grams",
    )(start, panels)


def fetch_kernel(which_ref, start_ref, panel_ref, start_out, high_out, low_out):
    high, low = split(panel_ref[0])
    start_out[0] = start_ref[0]
    high_out[0] = high
    low_out[0] = low


def fetched_blocks(which, start, panels):
    count = which.shape[0]
    eigen, columns = start.shape[2], panels.shape[2]

    def named(width):
        return pl.BlockSpec((1, BLOCK, width), lambda t, which: (0, which[t], 0))

    def kept(width):
        return pl.BlockSpec((1, BLOCK, width), lambda t, which: (t, 0, 0))

    return pl.pallas_call(
        fetch_kernel,
        out_shape=(
            jax.ShapeDtypeStruct((count, BLOCK, eigen), F32),
            jax.ShapeDtypeStruct((count, BLOCK, columns), BF16),
            jax.ShapeDtypeStruct((count, BLOCK, columns), BF16),
        ),
        grid_spec=pltpu.PrefetchScalarGridSpec(
            num_scalar_prefetch=1,
            grid=(count,),
            in_specs=[named(eigen), named(columns)],
            out_specs=(kept(eigen), kept(columns), kept(columns)),
        ),
        compiler_params=pltpu.CompilerParams(vmem_limit_bytes=10 << 20),
        cost_estimate=pl.CostEstimate(
            flops=count * BLOCK * columns,
            bytes_accessed=8 * count * BLOCK * (columns + eigen),
            transcendentals=0,
        ),
        name="fetch",
    )(which, start, panels)


def updated_block(start, panels, upper, lower, limit):
    high, low = panels
    back = start - (dot(high, upper) + (dot(high, lower) + dot(low, upper)))
    line = lax.broadcasted_iota(jnp.int32, back.shape, 0)
    return jnp.where(line < limit, back, 0.0).astype(BF16)


def solve_kernel(
    want_ref,
    limit_ref,
    sums_ref,
    exponent_ref,
    factor_ref,
    start_ref,
    high_ref,
    low_ref,
    out_ref,
    upper,
    lower,
):
    count = sums_ref.shape[0]
    width = factor_ref.shape[2]
    scale = jnp.exp2(exponent_ref[:1, :])
    size = (count * HALF, 128)
    inner = split(
        jnp.concatenate(
            [
                sums_ref[:, :HALF, :].reshape(size) * scale,
                sums_ref[:, HALF:PROJ, :].reshape(size) * scale,
            ],
            axis=1,
        )
    )
    links = split(sums_ref[:, PROJ:BODY, :].reshape(count * COUP, 128))

    def part(pair, k):
        return tuple(p[k * width : (k + 1) * width] for p in pair)

    factors = [split(factor_ref[0, level]) for level in range(4)]
    current = [dot3(factors[level], part(inner, level)) for level in range(4)]
    places = {3: ((0, 3), (1, 4), (2, 5)), 2: ((0, 0), (1, 1)), 1: ((0, 2),)}
    chained = {}
    for later, pairs in places.items():
        chained[later] = split(
            jnp.concatenate([dot3(factors[k], part(links, at)) for k, at in pairs], axis=0)
        )
    parts = [None] * 4
    for level in (3, 2, 1, 0):
        parts[level] = split(current[level])
        if level:
            moved = dot3(chained[level], parts[level])
            for k in range(level):
                current[k] = current[k] - moved[k * width : (k + 1) * width]
    upper[...] = jnp.concatenate([p[0] for p in parts], axis=0)
    lower[...] = jnp.concatenate([p[1] for p in parts], axis=0)
    for t in range(out_ref.shape[0]):
        out_ref[t] = updated_block(
            start_ref[t], (high_ref[t], low_ref[t]), upper[...], lower[...], limit_ref[want_ref[t]]
        )


def left_kernel(
    left_ref, occupied_ref, limit_ref, upper, lower, start_ref, panel_ref, out_ref
):
    turn = pl.program_id(0)
    out_ref[0] = updated_block(
        start_ref[0],
        split(panel_ref[0]),
        upper[...],
        lower[...],
        limit_ref[left_ref[turn]] * occupied_ref[turn],
    )


SCALARS = pl.BlockSpec(memory_space=pltpu.SMEM)
ARRAY = pl.BlockSpec(memory_space=pltpu.VMEM)


def update_cost(blocks, columns, eigen):
    return pl.CostEstimate(
        flops=6 * blocks * BLOCK * columns * eigen,
        bytes_accessed=4 * blocks * BLOCK * (columns + eigen),
        transcendentals=0,
    )


def solve_and_update(want, limits, sums, exponent, factors, start, high, low):
    count = want.shape[0]
    eigen, columns = start.shape[2], high.shape[2]
    coefficients = jax.ShapeDtypeStruct((columns, eigen), BF16)
    return pl.pallas_call(
        solve_kernel,
        out_shape=(
            jax.ShapeDtypeStruct((count, BLOCK, eigen), BF16),
            coefficients,
            coefficients,
        ),
        in_specs=[SCALARS] * 2 + [ARRAY] * 6,
        out_specs=(ARRAY,) * 3,
        compiler_params=pltpu.CompilerParams(vmem_limit_bytes=12 << 20),
        cost_estimate=update_cost(count, columns, eigen),
        name="solve",
    )(want, limits, sums, exponent, factors, start, high, low)


def left_blocks(left, occupied, limits, upper, lower, start, panels):
    count = left.shape[0]
    eigen, columns = start.shape[2], panels.shape[2]

    def named(width):
        return pl.BlockSpec((1, BLOCK, width), lambda t, which, *_: (0, which[t], 0))

    def whole(shape):
        return pl.BlockSpec(shape, lambda t, *_: (0, 0))

    return pl.pallas_call(
        left_kernel,
        out_shape=jax.ShapeDtypeStruct((count, BLOCK, eigen), BF16),
        grid_spec=pltpu.PrefetchScalarGridSpec(
            num_scalar_prefetch=3,
            grid=(count,),
            in_specs=[
                whole((columns, eigen)),
                whole((columns, eigen)),
                named(eigen),
                named(columns),
            ],
            out_specs=pl.BlockSpec((1, BLOCK, eigen), lambda t, *_: (t, 0, 0)),
        ),
        compiler_params=pltpu.CompilerParams(vmem_limit_bytes=16 << 20),
        cost_estimate=update_cost(count, columns, eigen),
        name="left",
    )(left, occupied, limits, upper, lower, start, panels)


def dipole_kernel(tile_ref, right_ref, left_ref, out_ref):
    total = None
    for t in range(tile_ref.shape[1]):
        product = dot(tile_ref[0, t], right_ref[t]).astype(BF16)
        term = dot(left_ref[t], product, ((0,), (0,)))
        total = term if total is None else total + term
    out_ref[...] = total.astype(BF16)


def tile_products(tiles, right, left):
    eigen = right.shape[2]
    return pl.pallas_call(
        dipole_kernel,
        out_shape=jax.ShapeDtypeStruct((eigen, eigen), BF16),
        compiler_params=pltpu.CompilerParams(vmem_limit_bytes=8 << 20),
        name="dipole",
    )(tiles, right, left)


def passed_along(block, axis, distance):
    devices = range(lax.axis_size(axis))
    route = [((i - distance) % len(devices), i) for i in devices]
    return lax.ppermute(block, axis, route)


def exchanged(shares, groups=None):
    return lax.all_to_all(shares, "row", 0, 0, axis_index_groups=groups, tiled=True)


def combined(terms):
    count = terms.shape[0]
    terms = terms.astype(F32)
    exponents = terms[:, BODY:]
    proj = jnp.sum(terms[:, :PROJ] * jnp.exp2(exponents[:, :1]), axis=0)
    coup = jnp.sum(terms[:, PROJ:BODY], axis=0) * (1.0 / count)
    exponent = jnp.max(exponents, axis=0) + float(count.bit_length() - 1)
    return jnp.concatenate([proj * jnp.exp2(-exponent[:1]), coup, exponent], axis=0)


def added(shares):
    exponents = [share[BODY:] for share in shares]
    proj = sum(s[:PROJ] * jnp.exp2(e[:1]) for s, e in zip(shares, exponents))
    coup = sum(s[PROJ:BODY] for s in shares) * (1.0 / len(shares))
    exponent = functools.reduce(jnp.maximum, exponents)
    exponent = exponent + float(len(shares).bit_length() - 1)
    return jnp.concatenate([proj * jnp.exp2(-exponent[:1]), coup, exponent], axis=0)


def around(share, step):
    count = lax.axis_size("row")
    route = [((i + step) % count, i) for i in range(count)]
    return lax.ppermute(share, "row", route)


def on_device(
    vectors, reflectors, factors, tiles, tile_left, tile_right, tile_occupied_mask, channels
):
    count = lax.axis_size("row")
    vectors = pltpu.with_memory_space_constraint(vectors, pltpu.HBM)
    reflectors = pltpu.with_memory_space_constraint(reflectors, pltpu.HBM)
    want = passed_along(tile_right[0], "sym", 1)
    far = count // NEAR
    inside = [[far_at * NEAR + at for at in range(NEAR)] for far_at in range(far)]
    shares = local_grams(vectors, reflectors, NEAR).astype(F16)
    want, shares = lax.optimization_barrier((want, shares))
    owned = combined(exchanged(shares, inside)).astype(F16)
    want, owned = lax.optimization_barrier((want, owned))
    named = fetched_blocks(want, vectors, reflectors)
    others = [around(owned, NEAR * step) for step in (1, far - 1, *range(2, far - 1))]
    others, named = lax.optimization_barrier((others, named))
    owned = added([share.astype(F32) for share in (owned, *others)])
    copies = jnp.broadcast_to(owned[:BODY].astype(F16), (NEAR, BODY, 128))
    sums = exchanged(copies, inside).astype(F32)
    exponent = owned[BODY:]
    packed, upper, lower = solve_and_update(
        want, channels[0], sums, exponent, factors, *named
    )
    right = passed_along(packed, "sym", -1)
    left = left_blocks(
        tile_left[0], tile_occupied_mask[0], channels[0], upper, lower, vectors, reflectors
    )
    partial = tile_products(tiles, right, left)
    eigen = partial.shape[1]
    owned = exchanged(partial.reshape(count, eigen // count, eigen))
    return jnp.sum(owned.astype(F32), axis=0)[None]


def solution(mesh):
    return jax.shard_map(
        on_device,
        mesh=mesh,
        in_specs=(
            P("sym", "row", None),
            P("sym", "row", None),
            P("sym", None, None, None),
            P("sym", "row", None, None),
            P("sym", "row"),
            P("sym", "row"),
            P("sym", "row"),
            P("sym", "row"),
        ),
        out_specs=P("sym", "row", None),
        check_vma=False,
    )
```

```python
import functools

import jax
import jax.numpy as jnp
from jax import lax
from jax.experimental import pallas as pl
from jax.experimental.pallas import tpu as pltpu
from jax.sharding import PartitionSpec as P

F32 = jnp.float32
BF16 = jnp.bfloat16
F16 = jnp.float16
BLOCK = 512
STEP = 1024
NEAR = 8
HALF = 64
PROJ = 2 * HALF
COUP = 96
BODY = PROJ + COUP
SHARE = BODY + 8
COUPLING_SCALE = 32.0
ROWS = ((0,), (0,))
PLAIN = ((1,), (0,))


def split(x):
    high = x.astype(BF16)
    return high, (x - high.astype(F32)).astype(BF16)


def dot(a, b, dims=PLAIN):
    return lax.dot_general(a, b, (dims, ((), ())), preferred_element_type=F32)


def dot3(a, b, dims=PLAIN):
    (ah, al), (bh, bl) = a, b
    return dot(ah, bh, dims) + (dot(ah, bl, dims) + dot(al, bh, dims))


def gram_kernel(start_ref, panel_ref, out_ref, proj, coup):
    step = pl.program_id(0)

    @pl.when(step == 0)
    def _():
        proj[...] = jnp.zeros_like(proj)
        coup[...] = jnp.zeros_like(coup)

    panels = split(panel_ref[0])
    start = split(start_ref[0])
    width = panel_ref.shape[2] // 4

    def columns(*which):
        return tuple(
            jnp.concatenate([p[:, k * width : (k + 1) * width] for k in which], axis=1)
            for p in panels
        )

    proj[...] += dot3(panels, start, ROWS)
    for place, (one, pair) in enumerate(((0, (1, 2)), (1, (2, 3)), (3, (2, 0)))):
        coup[place * width : (place + 1) * width] += dot3(
            columns(one), columns(*pair), ROWS
        )

    @pl.when(step == pl.num_programs(0) - 1)
    def _():
        inner = proj[...]
        top = jnp.max(jnp.abs(inner), axis=(0, 1), keepdims=True)
        exponent = jnp.ceil(jnp.log2(jnp.maximum(top, 1e-30))) - 14.0
        inner = inner * jnp.exp2(-exponent)
        count = out_ref.shape[0]
        out_ref[:, :HALF, :] = inner[:, :128].reshape(count, HALF, 128)
        out_ref[:, HALF:PROJ, :] = inner[:, 128:].reshape(count, HALF, 128)
        lines = jnp.concatenate([coup[:, :width], coup[:, width:]], axis=0)
        lines = lines * COUPLING_SCALE
        out_ref[:, PROJ:BODY, :] = lines.reshape(count, COUP, 128)
        out_ref[:, BODY:, :] = jnp.broadcast_to(
            exponent.reshape(1, 1, 1), (count, 8, 128)
        )


def local_grams(start, panels, count):
    rows, eigen = start.shape[1:]
    columns = panels.shape[2]
    return pl.pallas_call(
        gram_kernel,
        out_shape=jax.ShapeDtypeStruct((count, SHARE, 128), F32),
        grid=(rows // STEP,),
        in_specs=[
            pl.BlockSpec((1, STEP, eigen), lambda i: (0, i, 0)),
            pl.BlockSpec((1, STEP, columns), lambda i: (0, i, 0)),
        ],
        out_specs=pl.BlockSpec((count, SHARE, 128), lambda i: (0, 0, 0)),
        scratch_shapes=[
            pltpu.VMEM((columns, eigen), F32),
            pltpu.VMEM((3 * columns // 4, columns // 2), F32),
        ],
        compiler_params=pltpu.CompilerParams(vmem_limit_bytes=40 << 20),
        cost_estimate=pl.CostEstimate(
            flops=6 * rows * columns * (eigen + columns // 2),
            bytes_accessed=4 * rows * (eigen + columns),
            transcendentals=0,
        ),
        name="grams",
    )(start, panels)


def fetch_kernel(which_ref, start_ref, panel_ref, start_out, high_out, low_out):
    high, low = split(panel_ref[0])
    start_out[0] = start_ref[0]
    high_out[0] = high
    low_out[0] = low


def fetched_blocks(which, start, panels):
    count = which.shape[0]
    eigen, columns = start.shape[2], panels.shape[2]

    def named(width):
        return pl.BlockSpec((1, BLOCK, width), lambda t, which: (0, which[t], 0))

    def kept(width):
        return pl.BlockSpec((1, BLOCK, width), lambda t, which: (t, 0, 0))

    return pl.pallas_call(
        fetch_kernel,
        out_shape=(
            jax.ShapeDtypeStruct((count, BLOCK, eigen), F32),
            jax.ShapeDtypeStruct((count, BLOCK, columns), BF16),
            jax.ShapeDtypeStruct((count, BLOCK, columns), BF16),
        ),
        grid_spec=pltpu.PrefetchScalarGridSpec(
            num_scalar_prefetch=1,
            grid=(count,),
            in_specs=[named(eigen), named(columns)],
            out_specs=(kept(eigen), kept(columns), kept(columns)),
        ),
        compiler_params=pltpu.CompilerParams(vmem_limit_bytes=10 << 20),
        cost_estimate=pl.CostEstimate(
            flops=count * BLOCK * columns,
            bytes_accessed=8 * count * BLOCK * (columns + eigen),
            transcendentals=0,
        ),
        name="fetch",
    )(which, start, panels)


def updated_block(start, panels, upper, lower, limit):
    high, low = panels
    back = start - (dot(high, upper) + (dot(high, lower) + dot(low, upper)))
    line = lax.broadcasted_iota(jnp.int32, back.shape, 0)
    return jnp.where(line < limit, back, 0.0).astype(BF16)


def solve_kernel(
    want_ref,
    limit_ref,
    sums_ref,
    exponent_ref,
    factor_ref,
    start_ref,
    high_ref,
    low_ref,
    out_ref,
    upper,
    lower,
):
    count = sums_ref.shape[0]
    width = factor_ref.shape[2]
    scale = jnp.exp2(exponent_ref[:1, :])
    size = (count * HALF, 128)
    inner = split(
        jnp.concatenate(
            [
                sums_ref[:, :HALF, :].reshape(size) * scale,
                sums_ref[:, HALF:PROJ, :].reshape(size) * scale,
            ],
            axis=1,
        )
    )
    links = split(sums_ref[:, PROJ:BODY, :].reshape(count * COUP, 128))

    def part(pair, k):
        return tuple(p[k * width : (k + 1) * width] for p in pair)

    factors = [split(factor_ref[0, level]) for level in range(4)]
    current = [dot3(factors[level], part(inner, level)) for level in range(4)]
    turned = ((1,), (1,))
    places = {
        3: ((0, 5, turned), (1, 4, PLAIN), (2, 2, turned)),
        2: ((0, 3, PLAIN), (1, 1, PLAIN)),
        1: ((0, 0, PLAIN),),
    }
    chained = {}
    for later, entries in places.items():
        products = [dot3(factors[k], part(links, at), dims) for k, at, dims in entries]
        chained[later] = split(jnp.concatenate(products, axis=0))
    parts = [None] * 4
    for level in (3, 2, 1, 0):
        parts[level] = split(current[level])
        if level:
            moved = dot3(chained[level], parts[level])
            for k in range(level):
                current[k] = current[k] - moved[k * width : (k + 1) * width]
    upper[...] = jnp.concatenate([p[0] for p in parts], axis=0)
    lower[...] = jnp.concatenate([p[1] for p in parts], axis=0)
    for t in range(out_ref.shape[0]):
        out_ref[t] = updated_block(
            start_ref[t], (high_ref[t], low_ref[t]), upper[...], lower[...], limit_ref[want_ref[t]]
        )


def left_kernel(
    left_ref,
    occupied_ref,
    limit_ref,
    upper,
    lower,
    start_ref,
    panel_ref,
    tile_ref,
    high_out,
    low_out,
):
    turn = pl.program_id(0)
    block = updated_block(
        start_ref[0],
        split(panel_ref[0]),
        upper[...],
        lower[...],
        limit_ref[left_ref[turn]] * occupied_ref[turn],
    )
    high_out[...], low_out[...] = split(dot(block, tile_ref[0, 0], ROWS))


SCALARS = pl.BlockSpec(memory_space=pltpu.SMEM)
ARRAY = pl.BlockSpec(memory_space=pltpu.VMEM)


def update_cost(blocks, columns, eigen):
    return pl.CostEstimate(
        flops=6 * blocks * BLOCK * columns * eigen,
        bytes_accessed=4 * blocks * BLOCK * (columns + eigen),
        transcendentals=0,
    )


def solve_and_update(want, limits, sums, exponent, factors, start, high, low):
    count = want.shape[0]
    eigen, columns = start.shape[2], high.shape[2]
    coefficients = jax.ShapeDtypeStruct((columns, eigen), BF16)
    return pl.pallas_call(
        solve_kernel,
        out_shape=(
            jax.ShapeDtypeStruct((count, BLOCK, eigen), BF16),
            coefficients,
            coefficients,
        ),
        in_specs=[SCALARS] * 2 + [ARRAY] * 6,
        out_specs=(ARRAY,) * 3,
        compiler_params=pltpu.CompilerParams(vmem_limit_bytes=12 << 20),
        cost_estimate=update_cost(count, columns, eigen),
        name="solve",
    )(want, limits, sums, exponent, factors, start, high, low)


def left_products(left, occupied, limits, upper, lower, start, panels, tiles):
    count = left.shape[0]
    eigen, columns = start.shape[2], panels.shape[2]

    def named(width):
        return pl.BlockSpec((1, BLOCK, width), lambda t, which, *_: (0, which[t], 0))

    def whole(shape):
        return pl.BlockSpec(shape, lambda t, *_: (0, 0))

    wide = pl.BlockSpec((eigen, BLOCK), lambda t, *_: (0, t))
    return pl.pallas_call(
        left_kernel,
        out_shape=(jax.ShapeDtypeStruct((eigen, count * BLOCK), BF16),) * 2,
        grid_spec=pltpu.PrefetchScalarGridSpec(
            num_scalar_prefetch=3,
            grid=(count,),
            in_specs=[
                whole((columns, eigen)),
                whole((columns, eigen)),
                named(eigen),
                named(columns),
                pl.BlockSpec((1, 1, BLOCK, BLOCK), lambda t, *_: (0, t, 0, 0)),
            ],
            out_specs=(wide, wide),
        ),
        compiler_params=pltpu.CompilerParams(vmem_limit_bytes=16 << 20),
        cost_estimate=update_cost(count, columns, eigen),
        name="left",
    )(left, occupied, limits, upper, lower, start, panels, tiles)


def dipole_kernel(high_ref, low_ref, right_ref, out_ref):
    right = right_ref[...].reshape(-1, right_ref.shape[2])
    out_ref[...] = (dot(high_ref[...], right) + dot(low_ref[...], right)).astype(BF16)


def tile_products(high, low, right):
    eigen = right.shape[2]
    return pl.pallas_call(
        dipole_kernel,
        out_shape=jax.ShapeDtypeStruct((eigen, eigen), BF16),
        in_specs=[ARRAY] * 3,
        out_specs=ARRAY,
        compiler_params=pltpu.CompilerParams(vmem_limit_bytes=8 << 20),
        name="dipole",
    )(high, low, right)


def passed_along(block, axis, distance):
    devices = range(lax.axis_size(axis))
    route = [((i - distance) % len(devices), i) for i in devices]
    return lax.ppermute(block, axis, route)


def exchanged(shares, groups=None):
    return lax.all_to_all(shares, "row", 0, 0, axis_index_groups=groups, tiled=True)


def combined(terms):
    count = terms.shape[0]
    terms = terms.astype(F32)
    exponents = terms[:, BODY:]
    proj = jnp.sum(terms[:, :PROJ] * jnp.exp2(exponents[:, :1]), axis=0)
    coup = jnp.sum(terms[:, PROJ:BODY], axis=0) * (1.0 / count)
    exponent = jnp.max(exponents, axis=0) + float(count.bit_length() - 1)
    return jnp.concatenate([proj * jnp.exp2(-exponent[:1]), coup, exponent], axis=0)


def added(shares):
    exponents = [share[BODY:] for share in shares]
    proj = sum(s[:PROJ] * jnp.exp2(e[:1]) for s, e in zip(shares, exponents))
    coup = sum(s[PROJ:BODY] for s in shares) * (1.0 / len(shares))
    exponent = functools.reduce(jnp.maximum, exponents)
    exponent = exponent + float(len(shares).bit_length() - 1)
    return jnp.concatenate([proj * jnp.exp2(-exponent[:1]), coup, exponent], axis=0)


def around(share, step):
    count = lax.axis_size("row")
    route = [((i + step) % count, i) for i in range(count)]
    return lax.ppermute(share, "row", route)


def on_device(
    vectors, reflectors, factors, tiles, tile_left, tile_right, tile_occupied_mask, channels
):
    count = lax.axis_size("row")
    vectors = pltpu.with_memory_space_constraint(vectors, pltpu.HBM)
    reflectors = pltpu.with_memory_space_constraint(reflectors, pltpu.HBM)
    want = passed_along(tile_right[0], "sym", 1)
    far = count // NEAR
    inside = [[far_at * NEAR + at for at in range(NEAR)] for far_at in range(far)]
    shares = local_grams(vectors, reflectors, NEAR).astype(F16)
    want, shares = lax.optimization_barrier((want, shares))
    owned = combined(exchanged(shares, inside)).astype(F16)
    want, owned = lax.optimization_barrier((want, owned))
    named = fetched_blocks(want, vectors, reflectors)
    others = [around(owned, NEAR * step) for step in (1, far - 1, *range(2, far - 1))]
    others, named = lax.optimization_barrier((others, named))
    owned = added([share.astype(F32) for share in (owned, *others)])
    copies = jnp.broadcast_to(owned[:BODY].astype(F16), (NEAR, BODY, 128))
    sums = exchanged(copies, inside).astype(F32)
    exponent = owned[BODY:]
    packed, upper, lower = solve_and_update(
        want, channels[0], sums, exponent, factors, *named
    )
    right = passed_along(packed, "sym", -1)
    left = left_products(
        tile_left[0],
        tile_occupied_mask[0],
        channels[0],
        upper,
        lower,
        vectors,
        reflectors,
        tiles,
    )
    partial = tile_products(*left, right)
    eigen = partial.shape[1]
    owned = exchanged(partial.reshape(count, eigen // count, eigen))
    return jnp.sum(owned.astype(F32), axis=0)[None]


def solution(mesh):
    return jax.shard_map(
        on_device,
        mesh=mesh,
        in_specs=(
            P("sym", "row", None),
            P("sym", "row", None),
            P("sym", None, None, None),
            P("sym", "row", None, None),
            P("sym", "row"),
            P("sym", "row"),
            P("sym", "row"),
            P("sym", "row"),
        ),
        out_specs=P("sym", "row", None),
        check_vma=False,
    )
```

```python
import functools

import jax
import jax.numpy as jnp
from jax import lax
from jax.experimental import pallas as pl
from jax.experimental.pallas import tpu as pltpu
from jax.sharding import PartitionSpec as P

F32 = jnp.float32
BF16 = jnp.bfloat16
F16 = jnp.float16
BLOCK = 512
STEP = 1024
NEAR = 8
HALF = 64
PROJ = 2 * HALF
COUP = 96
BODY = PROJ + COUP
SHARE = BODY + 8
COUPLING_SCALE = 32.0
ROWS = ((0,), (0,))
PLAIN = ((1,), (0,))


def split(x):
    high = x.astype(BF16)
    return high, (x - high.astype(F32)).astype(BF16)


def dot(a, b, dims=PLAIN):
    return lax.dot_general(a, b, (dims, ((), ())), preferred_element_type=F32)


def dot3(a, b, dims=PLAIN):
    (ah, al), (bh, bl) = a, b
    return dot(ah, bh, dims) + (dot(ah, bl, dims) + dot(al, bh, dims))


def gram_kernel(start_ref, panel_ref, out_ref, proj, coup):
    step = pl.program_id(0)

    @pl.when(step == 0)
    def _():
        proj[...] = jnp.zeros_like(proj)
        coup[...] = jnp.zeros_like(coup)

    panels = split(panel_ref[0])
    start = split(start_ref[0])
    width = panel_ref.shape[2] // 4

    def columns(*which):
        return tuple(
            jnp.concatenate([p[:, k * width : (k + 1) * width] for k in which], axis=1)
            for p in panels
        )

    proj[...] += dot3(panels, start, ROWS)
    for place, (one, pair) in enumerate(((0, (1, 2)), (1, (2, 3)), (3, (2, 0)))):
        coup[place * width : (place + 1) * width] += dot3(
            columns(one), columns(*pair), ROWS
        )

    @pl.when(step == pl.num_programs(0) - 1)
    def _():
        inner = proj[...]
        top = jnp.max(jnp.abs(inner), axis=(0, 1), keepdims=True)
        exponent = jnp.ceil(jnp.log2(jnp.maximum(top, 1e-30))) - 14.0
        inner = inner * jnp.exp2(-exponent)
        count = out_ref.shape[0]
        out_ref[:, :HALF, :] = inner[:, :128].reshape(count, HALF, 128)
        out_ref[:, HALF:PROJ, :] = inner[:, 128:].reshape(count, HALF, 128)
        lines = jnp.concatenate([coup[:, :width], coup[:, width:]], axis=0)
        lines = lines * COUPLING_SCALE
        out_ref[:, PROJ:BODY, :] = lines.reshape(count, COUP, 128)
        out_ref[:, BODY:, :] = jnp.broadcast_to(
            exponent.reshape(1, 1, 1), (count, 8, 128)
        )


def local_grams(start, panels, count):
    rows, eigen = start.shape[1:]
    columns = panels.shape[2]
    return pl.pallas_call(
        gram_kernel,
        out_shape=jax.ShapeDtypeStruct((count, SHARE, 128), F32),
        grid=(rows // STEP,),
        in_specs=[
            pl.BlockSpec((1, STEP, eigen), lambda i: (0, i, 0)),
            pl.BlockSpec((1, STEP, columns), lambda i: (0, i, 0)),
        ],
        out_specs=pl.BlockSpec((count, SHARE, 128), lambda i: (0, 0, 0)),
        scratch_shapes=[
            pltpu.VMEM((columns, eigen), F32),
            pltpu.VMEM((3 * columns // 4, columns // 2), F32),
        ],
        compiler_params=pltpu.CompilerParams(vmem_limit_bytes=40 << 20),
        cost_estimate=pl.CostEstimate(
            flops=6 * rows * columns * (eigen + columns // 2),
            bytes_accessed=4 * rows * (eigen + columns),
            transcendentals=0,
        ),
        name="grams",
    )(start, panels)


def fetch_kernel(which_ref, start_ref, panel_ref, start_out, high_out, low_out):
    high, low = split(panel_ref[0])
    start_out[0] = start_ref[0]
    high_out[0] = high
    low_out[0] = low


def fetched_blocks(which, start, panels):
    count = which.shape[0]
    eigen, columns = start.shape[2], panels.shape[2]

    def named(width):
        return pl.BlockSpec((1, BLOCK, width), lambda t, which: (0, which[t], 0))

    def kept(width):
        return pl.BlockSpec((1, BLOCK, width), lambda t, which: (t, 0, 0))

    return pl.pallas_call(
        fetch_kernel,
        out_shape=(
            jax.ShapeDtypeStruct((count, BLOCK, eigen), F32),
            jax.ShapeDtypeStruct((count, BLOCK, columns), BF16),
            jax.ShapeDtypeStruct((count, BLOCK, columns), BF16),
        ),
        grid_spec=pltpu.PrefetchScalarGridSpec(
            num_scalar_prefetch=1,
            grid=(count,),
            in_specs=[named(eigen), named(columns)],
            out_specs=(kept(eigen), kept(columns), kept(columns)),
        ),
        compiler_params=pltpu.CompilerParams(vmem_limit_bytes=10 << 20),
        cost_estimate=pl.CostEstimate(
            flops=count * BLOCK * columns,
            bytes_accessed=8 * count * BLOCK * (columns + eigen),
            transcendentals=0,
        ),
        name="fetch",
    )(which, start, panels)


def updated_block(start, panels, upper, lower, limits):
    high, low = panels
    back = start - (dot(high, upper) + (dot(high, lower) + dot(low, upper)))
    line = lax.broadcasted_iota(jnp.int32, (BLOCK, back.shape[1]), 0)
    live = jnp.concatenate([line < limit for limit in limits], axis=0)
    return jnp.where(live, back, 0.0).astype(BF16)


def solve_kernel(
    want_ref,
    limit_ref,
    sums_ref,
    exponent_ref,
    factor_ref,
    start_ref,
    high_ref,
    low_ref,
    out_ref,
    upper,
    lower,
):
    count = sums_ref.shape[0]
    width = factor_ref.shape[2]
    scale = jnp.exp2(exponent_ref[:1, :])
    size = (count * HALF, 128)
    inner = split(
        jnp.concatenate(
            [
                sums_ref[:, :HALF, :].reshape(size) * scale,
                sums_ref[:, HALF:PROJ, :].reshape(size) * scale,
            ],
            axis=1,
        )
    )
    links = split(sums_ref[:, PROJ:BODY, :].reshape(count * COUP, 128))

    def part(pair, k):
        return tuple(p[k * width : (k + 1) * width] for p in pair)

    factors = [split(factor_ref[0, level]) for level in range(4)]
    current = [dot3(factors[level], part(inner, level)) for level in range(4)]
    turned = ((1,), (1,))
    places = {
        3: ((0, 5, turned), (1, 4, PLAIN), (2, 2, turned)),
        2: ((0, 3, PLAIN), (1, 1, PLAIN)),
        1: ((0, 0, PLAIN),),
    }
    chained = {}
    for later, entries in places.items():
        products = [dot3(factors[k], part(links, at), dims) for k, at, dims in entries]
        chained[later] = split(jnp.concatenate(products, axis=0))
    parts = [None] * 4
    for level in (3, 2, 1, 0):
        parts[level] = split(current[level])
        if level:
            moved = dot3(chained[level], parts[level])
            for k in range(level):
                current[k] = current[k] - moved[k * width : (k + 1) * width]
    upper[...] = jnp.concatenate([p[0] for p in parts], axis=0)
    lower[...] = jnp.concatenate([p[1] for p in parts], axis=0)
    shape = out_ref.shape
    limits = [limit_ref[want_ref[t]] for t in range(shape[0])]
    tall = (shape[0] * shape[1], -1)
    out_ref[...] = updated_block(
        start_ref[...].reshape(tall),
        (high_ref[...].reshape(tall), low_ref[...].reshape(tall)),
        upper[...],
        lower[...],
        limits,
    ).reshape(shape)


def left_kernel(
    left_ref,
    occupied_ref,
    limit_ref,
    upper,
    lower,
    start_ref,
    panel_ref,
    tile_ref,
    high_out,
    low_out,
):
    turn = pl.program_id(0)
    block = updated_block(
        start_ref[0],
        split(panel_ref[0]),
        upper[...],
        lower[...],
        [limit_ref[left_ref[turn]] * occupied_ref[turn]],
    )
    high_out[...], low_out[...] = split(dot(block, tile_ref[0, 0], ROWS))


SCALARS = pl.BlockSpec(memory_space=pltpu.SMEM)
ARRAY = pl.BlockSpec(memory_space=pltpu.VMEM)


def update_cost(blocks, columns, eigen):
    return pl.CostEstimate(
        flops=6 * blocks * BLOCK * columns * eigen,
        bytes_accessed=4 * blocks * BLOCK * (columns + eigen),
        transcendentals=0,
    )


def solve_and_update(want, limits, sums, exponent, factors, start, high, low):
    count = want.shape[0]
    eigen, columns = start.shape[2], high.shape[2]
    coefficients = jax.ShapeDtypeStruct((columns, eigen), BF16)
    return pl.pallas_call(
        solve_kernel,
        out_shape=(
            jax.ShapeDtypeStruct((count, BLOCK, eigen), BF16),
            coefficients,
            coefficients,
        ),
        in_specs=[SCALARS] * 2 + [ARRAY] * 6,
        out_specs=(ARRAY,) * 3,
        compiler_params=pltpu.CompilerParams(vmem_limit_bytes=12 << 20),
        cost_estimate=update_cost(count, columns, eigen),
        name="solve",
    )(want, limits, sums, exponent, factors, start, high, low)


def left_products(left, occupied, limits, upper, lower, start, panels, tiles):
    count = left.shape[0]
    eigen, columns = start.shape[2], panels.shape[2]

    def named(width):
        return pl.BlockSpec((1, BLOCK, width), lambda t, which, *_: (0, which[t], 0))

    def whole(shape):
        return pl.BlockSpec(shape, lambda t, *_: (0, 0))

    wide = pl.BlockSpec((eigen, BLOCK), lambda t, *_: (0, t))
    return pl.pallas_call(
        left_kernel,
        out_shape=(jax.ShapeDtypeStruct((eigen, count * BLOCK), BF16),) * 2,
        grid_spec=pltpu.PrefetchScalarGridSpec(
            num_scalar_prefetch=3,
            grid=(count,),
            in_specs=[
                whole((columns, eigen)),
                whole((columns, eigen)),
                named(eigen),
                named(columns),
                pl.BlockSpec((1, 1, BLOCK, BLOCK), lambda t, *_: (0, t, 0, 0)),
            ],
            out_specs=(wide, wide),
        ),
        compiler_params=pltpu.CompilerParams(vmem_limit_bytes=16 << 20),
        cost_estimate=update_cost(count, columns, eigen),
        name="left",
    )(left, occupied, limits, upper, lower, start, panels, tiles)


def dipole_kernel(high_ref, low_ref, right_ref, out_ref):
    right = right_ref[...].reshape(-1, right_ref.shape[2])
    out_ref[...] = (dot(high_ref[...], right) + dot(low_ref[...], right)).astype(BF16)


def tile_products(high, low, right):
    eigen = right.shape[2]
    return pl.pallas_call(
        dipole_kernel,
        out_shape=jax.ShapeDtypeStruct((eigen, eigen), BF16),
        in_specs=[ARRAY] * 3,
        out_specs=ARRAY,
        compiler_params=pltpu.CompilerParams(vmem_limit_bytes=8 << 20),
        name="dipole",
    )(high, low, right)


def passed_along(block, axis, distance):
    devices = range(lax.axis_size(axis))
    route = [((i - distance) % len(devices), i) for i in devices]
    return lax.ppermute(block, axis, route)


def exchanged(shares, groups=None):
    return lax.all_to_all(shares, "row", 0, 0, axis_index_groups=groups, tiled=True)


def combined(shares):
    shares = [share.astype(F32) for share in shares]
    exponents = [share[BODY:] for share in shares]
    exponent = functools.reduce(jnp.maximum, exponents)
    exponent = exponent + float(len(shares).bit_length() - 1)
    proj = sum(
        share[:PROJ] * jnp.exp2(own[:1] - exponent[:1])
        for share, own in zip(shares, exponents)
    )
    coup = sum(share[PROJ:BODY] for share in shares) * (1.0 / len(shares))
    return jnp.concatenate([proj, coup], axis=0), exponent


def around(share, step):
    count = lax.axis_size("row")
    route = [((i + step) % count, i) for i in range(count)]
    return lax.ppermute(share, "row", route)


def on_device(
    vectors, reflectors, factors, tiles, tile_left, tile_right, tile_occupied_mask, channels
):
    count = lax.axis_size("row")
    vectors = pltpu.with_memory_space_constraint(vectors, pltpu.HBM)
    reflectors = pltpu.with_memory_space_constraint(reflectors, pltpu.HBM)
    want = passed_along(tile_right[0], "sym", 1)
    far = count // NEAR
    inside = [[far_at * NEAR + at for at in range(NEAR)] for far_at in range(far)]
    shares = local_grams(vectors, reflectors, NEAR).astype(F16)
    want, shares = lax.optimization_barrier((want, shares))
    terms = exchanged(shares, inside)
    owned = jnp.concatenate(combined([terms[at] for at in range(NEAR)]), axis=0)
    owned = owned.astype(F16)
    want, owned = lax.optimization_barrier((want, owned))
    named = fetched_blocks(want, vectors, reflectors)
    others = [around(owned, NEAR * step) for step in (1, far - 1, *range(2, far - 1))]
    others, named = lax.optimization_barrier((others, named))
    body, exponent = combined([owned, *others])
    copies = jnp.broadcast_to(body.astype(F16), (NEAR, BODY, 128))
    sums = exchanged(copies, inside).astype(F32)
    packed, upper, lower = solve_and_update(
        want, channels[0], sums, exponent, factors, *named
    )
    right = passed_along(packed, "sym", -1)
    left = left_products(
        tile_left[0],
        tile_occupied_mask[0],
        channels[0],
        upper,
        lower,
        vectors,
        reflectors,
        tiles,
    )
    partial = tile_products(*left, right)
    eigen = partial.shape[1]
    owned = exchanged(partial.reshape(count, eigen // count, eigen))
    return jnp.sum(owned.astype(F32), axis=0)[None]


def solution(mesh):
    return jax.shard_map(
        on_device,
        mesh=mesh,
        in_specs=(
            P("sym", "row", None),
            P("sym", "row", None),
            P("sym", None, None, None),
            P("sym", "row", None, None),
            P("sym", "row"),
            P("sym", "row"),
            P("sym", "row"),
            P("sym", "row"),
        ),
        out_specs=P("sym", "row", None),
        check_vma=False,
    )
```

```python
import functools

import jax
import jax.numpy as jnp
from jax import lax
from jax.experimental import pallas as pl
from jax.experimental.pallas import tpu as pltpu
from jax.sharding import PartitionSpec as P

F32 = jnp.float32
BF16 = jnp.bfloat16
F16 = jnp.float16
BLOCK = 512
STEP = 1024
NEAR = 8
HALF = 64
PROJ = 2 * HALF
COUP = 96
BODY = PROJ + COUP
SHARE = BODY + 8
COUPLING_SCALE = 32.0
ROWS = ((0,), (0,))
PLAIN = ((1,), (0,))


def split(x):
    high = x.astype(BF16)
    return high, (x - high.astype(F32)).astype(BF16)


def dot(a, b, dims=PLAIN):
    return lax.dot_general(a, b, (dims, ((), ())), preferred_element_type=F32)


def dot3(a, b, dims=PLAIN):
    (ah, al), (bh, bl) = a, b
    return dot(ah, bh, dims) + (dot(ah, bl, dims) + dot(al, bh, dims))


def gram_kernel(start_ref, panel_ref, out_ref, proj, coup):
    step = pl.program_id(0)

    @pl.when(step == 0)
    def _():
        proj[...] = jnp.zeros_like(proj)
        coup[...] = jnp.zeros_like(coup)

    panels = split(panel_ref[0])
    start = split(start_ref[0])
    width = panel_ref.shape[2] // 4

    def columns(*which):
        return tuple(
            jnp.concatenate([p[:, k * width : (k + 1) * width] for k in which], axis=1)
            for p in panels
        )

    proj[...] += dot3(panels, start, ROWS)
    for place, (one, pair) in enumerate(((0, (1, 2)), (1, (2, 3)), (3, (2, 0)))):
        coup[place * width : (place + 1) * width] += dot3(
            columns(one), columns(*pair), ROWS
        )

    @pl.when(step == pl.num_programs(0) - 1)
    def _():
        inner = proj[...]
        top = jnp.max(jnp.abs(inner), axis=(0, 1), keepdims=True)
        exponent = jnp.ceil(jnp.log2(jnp.maximum(top, 1e-30))) - 14.0
        inner = inner * jnp.exp2(-exponent)
        count = out_ref.shape[0]
        out_ref[:, :HALF, :] = inner[:, :128].reshape(count, HALF, 128)
        out_ref[:, HALF:PROJ, :] = inner[:, 128:].reshape(count, HALF, 128)
        lines = jnp.concatenate([coup[:, :width], coup[:, width:]], axis=0)
        lines = lines * COUPLING_SCALE
        out_ref[:, PROJ:BODY, :] = lines.reshape(count, COUP, 128)
        out_ref[:, BODY:, :] = jnp.broadcast_to(
            exponent.reshape(1, 1, 1), (count, 8, 128)
        )


def local_grams(start, panels, count):
    rows, eigen = start.shape[1:]
    columns = panels.shape[2]
    return pl.pallas_call(
        gram_kernel,
        out_shape=jax.ShapeDtypeStruct((count, SHARE, 128), F32),
        grid=(rows // STEP,),
        in_specs=[
            pl.BlockSpec((1, STEP, eigen), lambda i: (0, i, 0)),
            pl.BlockSpec((1, STEP, columns), lambda i: (0, i, 0)),
        ],
        out_specs=pl.BlockSpec((count, SHARE, 128), lambda i: (0, 0, 0)),
        scratch_shapes=[
            pltpu.VMEM((columns, eigen), F32),
            pltpu.VMEM((3 * columns // 4, columns // 2), F32),
        ],
        compiler_params=pltpu.CompilerParams(vmem_limit_bytes=40 << 20),
        cost_estimate=pl.CostEstimate(
            flops=6 * rows * columns * (eigen + columns // 2),
            bytes_accessed=4 * rows * (eigen + columns),
            transcendentals=0,
        ),
        name="grams",
    )(start, panels)


def fetch_kernel(which_ref, start_ref, panel_ref, start_out, high_out, low_out):
    high, low = split(panel_ref[0])
    start_out[0] = start_ref[0]
    high_out[0] = high
    low_out[0] = low


def fetched_blocks(which, start, panels):
    count = which.shape[0]
    eigen, columns = start.shape[2], panels.shape[2]

    def named(width):
        return pl.BlockSpec((1, BLOCK, width), lambda t, which: (0, which[t], 0))

    def kept(width):
        return pl.BlockSpec((1, BLOCK, width), lambda t, which: (t, 0, 0))

    return pl.pallas_call(
        fetch_kernel,
        out_shape=(
            jax.ShapeDtypeStruct((count, BLOCK, eigen), F32),
            jax.ShapeDtypeStruct((count, BLOCK, columns), BF16),
            jax.ShapeDtypeStruct((count, BLOCK, columns), BF16),
        ),
        grid_spec=pltpu.PrefetchScalarGridSpec(
            num_scalar_prefetch=1,
            grid=(count,),
            in_specs=[named(eigen), named(columns)],
            out_specs=(kept(eigen), kept(columns), kept(columns)),
        ),
        compiler_params=pltpu.CompilerParams(vmem_limit_bytes=10 << 20),
        cost_estimate=pl.CostEstimate(
            flops=count * BLOCK * columns,
            bytes_accessed=8 * count * BLOCK * (columns + eigen),
            transcendentals=0,
        ),
        name="fetch",
    )(which, start, panels)


def updated_block(start, panels, upper, lower, limits):
    high, low = panels
    back = start - (dot(high, upper) + (dot(high, lower) + dot(low, upper)))
    line = lax.broadcasted_iota(jnp.int32, (BLOCK, back.shape[1]), 0)
    live = jnp.concatenate([line < limit for limit in limits], axis=0)
    return jnp.where(live, back, 0.0).astype(BF16)


def solve_kernel(
    want_ref,
    limit_ref,
    sums_ref,
    rests_ref,
    exponent_ref,
    factor_ref,
    start_ref,
    high_ref,
    low_ref,
    out_ref,
    upper,
    lower,
):
    width = factor_ref.shape[2]
    scale = jnp.exp2(exponent_ref[:1, :1])

    def lines(begin, end):
        return tuple(ref[:, begin:end, :].reshape(-1, 128) for ref in (sums_ref, rests_ref))

    inner = tuple(
        jnp.concatenate(pair, axis=1) for pair in zip(lines(0, HALF), lines(HALF, PROJ))
    )
    links = lines(PROJ, BODY)

    def part(pair, k):
        return tuple(p[k * width : (k + 1) * width] for p in pair)

    factors = [split(factor_ref[0, level]) for level in range(4)]
    current = [dot3(factors[level], part(inner, level)) * scale for level in range(4)]
    turned = ((1,), (1,))
    places = {
        3: ((0, 5, turned), (1, 4, PLAIN), (2, 2, turned)),
        2: ((0, 3, PLAIN), (1, 1, PLAIN)),
        1: ((0, 0, PLAIN),),
    }
    chained = {}
    for later, entries in places.items():
        products = [dot3(factors[k], part(links, at), dims) for k, at, dims in entries]
        chained[later] = split(jnp.concatenate(products, axis=0))
    parts = [None] * 4
    for level in (3, 2, 1, 0):
        parts[level] = split(current[level])
        if level:
            moved = dot3(chained[level], parts[level])
            for k in range(level):
                current[k] = current[k] - moved[k * width : (k + 1) * width]
    upper[...] = jnp.concatenate([p[0] for p in parts], axis=0)
    lower[...] = jnp.concatenate([p[1] for p in parts], axis=0)
    shape = out_ref.shape
    limits = [limit_ref[want_ref[t]] for t in range(shape[0])]
    tall = (shape[0] * shape[1], -1)
    out_ref[...] = updated_block(
        start_ref[...].reshape(tall),
        (high_ref[...].reshape(tall), low_ref[...].reshape(tall)),
        upper[...],
        lower[...],
        limits,
    ).reshape(shape)


def left_kernel(
    left_ref,
    occupied_ref,
    limit_ref,
    upper,
    lower,
    start_ref,
    panel_ref,
    tile_ref,
    high_out,
    low_out,
):
    turn = pl.program_id(0)
    block = updated_block(
        start_ref[0],
        split(panel_ref[0]),
        upper[...],
        lower[...],
        [limit_ref[left_ref[turn]] * occupied_ref[turn]],
    )
    high_out[...], low_out[...] = split(dot(block, tile_ref[0, 0], ROWS))


SCALARS = pl.BlockSpec(memory_space=pltpu.SMEM)
ARRAY = pl.BlockSpec(memory_space=pltpu.VMEM)


def update_cost(blocks, columns, eigen):
    return pl.CostEstimate(
        flops=6 * blocks * BLOCK * columns * eigen,
        bytes_accessed=4 * blocks * BLOCK * (columns + eigen),
        transcendentals=0,
    )


def solve_and_update(want, limits, sums, rests, exponent, factors, start, high, low):
    count = want.shape[0]
    eigen, columns = start.shape[2], high.shape[2]
    coefficients = jax.ShapeDtypeStruct((columns, eigen), BF16)
    return pl.pallas_call(
        solve_kernel,
        out_shape=(
            jax.ShapeDtypeStruct((count, BLOCK, eigen), BF16),
            coefficients,
            coefficients,
        ),
        in_specs=[SCALARS] * 2 + [ARRAY] * 7,
        out_specs=(ARRAY,) * 3,
        compiler_params=pltpu.CompilerParams(vmem_limit_bytes=12 << 20),
        cost_estimate=update_cost(count, columns, eigen),
        name="solve",
    )(want, limits, sums, rests, exponent, factors, start, high, low)


def left_products(left, occupied, limits, upper, lower, start, panels, tiles):
    count = left.shape[0]
    eigen, columns = start.shape[2], panels.shape[2]

    def named(width):
        return pl.BlockSpec((1, BLOCK, width), lambda t, which, *_: (0, which[t], 0))

    def whole(shape):
        return pl.BlockSpec(shape, lambda t, *_: (0, 0))

    wide = pl.BlockSpec((eigen, BLOCK), lambda t, *_: (0, t))
    return pl.pallas_call(
        left_kernel,
        out_shape=(jax.ShapeDtypeStruct((eigen, count * BLOCK), BF16),) * 2,
        grid_spec=pltpu.PrefetchScalarGridSpec(
            num_scalar_prefetch=3,
            grid=(count,),
            in_specs=[
                whole((columns, eigen)),
                whole((columns, eigen)),
                named(eigen),
                named(columns),
                pl.BlockSpec((1, 1, BLOCK, BLOCK), lambda t, *_: (0, t, 0, 0)),
            ],
            out_specs=(wide, wide),
        ),
        compiler_params=pltpu.CompilerParams(vmem_limit_bytes=16 << 20),
        cost_estimate=update_cost(count, columns, eigen),
        name="left",
    )(left, occupied, limits, upper, lower, start, panels, tiles)


def dipole_kernel(high_ref, low_ref, right_ref, out_ref):
    right = right_ref[...].reshape(-1, right_ref.shape[2])
    out_ref[...] = (dot(high_ref[...], right) + dot(low_ref[...], right)).astype(BF16)


def tile_products(high, low, right):
    eigen = right.shape[2]
    return pl.pallas_call(
        dipole_kernel,
        out_shape=jax.ShapeDtypeStruct((eigen, eigen), BF16),
        in_specs=[ARRAY] * 3,
        out_specs=ARRAY,
        compiler_params=pltpu.CompilerParams(vmem_limit_bytes=8 << 20),
        name="dipole",
    )(high, low, right)


def passed_along(block, axis, distance):
    devices = range(lax.axis_size(axis))
    route = [((i - distance) % len(devices), i) for i in devices]
    return lax.ppermute(block, axis, route)


def exchanged(shares, groups=None):
    return lax.all_to_all(shares, "row", 0, 0, axis_index_groups=groups, tiled=True)


def combined(shares):
    shares = [share.astype(F32) for share in shares]
    exponents = [share[BODY:] for share in shares]
    exponent = functools.reduce(jnp.maximum, exponents)
    exponent = exponent + float(len(shares).bit_length() - 1)
    proj = sum(
        share[:PROJ] * jnp.exp2(own[:1] - exponent[:1])
        for share, own in zip(shares, exponents)
    )
    coup = sum(share[PROJ:BODY] for share in shares) * (1.0 / len(shares))
    return jnp.concatenate([proj, coup], axis=0), exponent


def around(share, step):
    count = lax.axis_size("row")
    route = [((i + step) % count, i) for i in range(count)]
    return lax.ppermute(share, "row", route)


def on_device(
    vectors, reflectors, factors, tiles, tile_left, tile_right, tile_occupied_mask, channels
):
    count = lax.axis_size("row")
    vectors = pltpu.with_memory_space_constraint(vectors, pltpu.HBM)
    reflectors = pltpu.with_memory_space_constraint(reflectors, pltpu.HBM)
    want = passed_along(tile_right[0], "sym", 1)
    far = count // NEAR
    inside = [[far_at * NEAR + at for at in range(NEAR)] for far_at in range(far)]
    shares = local_grams(vectors, reflectors, NEAR).astype(F16)
    want, shares = lax.optimization_barrier((want, shares))
    terms = exchanged(shares, inside)
    owned = jnp.concatenate(combined([terms[at] for at in range(NEAR)]), axis=0)
    owned = owned.astype(F16)
    want, owned = lax.optimization_barrier((want, owned))
    named = fetched_blocks(want, vectors, reflectors)
    others = [around(owned, NEAR * step) for step in (1, far - 1, *range(2, far - 1))]
    others, named = lax.optimization_barrier((others, named))
    body, exponent = combined([owned, *others])
    copies = jnp.broadcast_to(body.astype(F16), (NEAR, BODY, 128))
    sums = exchanged(copies, inside).astype(F32)
    upper_sums = lax.reduce_precision(sums, exponent_bits=8, mantissa_bits=7)
    rests = (sums - upper_sums).astype(BF16)
    sums = upper_sums.astype(BF16)
    packed, upper, lower = solve_and_update(
        want, channels[0], sums, rests, exponent, factors, *named
    )
    right = passed_along(packed, "sym", -1)
    left = left_products(
        tile_left[0],
        tile_occupied_mask[0],
        channels[0],
        upper,
        lower,
        vectors,
        reflectors,
        tiles,
    )
    partial = tile_products(*left, right)
    eigen = partial.shape[1]
    owned = exchanged(partial.reshape(count, eigen // count, eigen))
    return jnp.sum(owned.astype(F32), axis=0)[None]


def solution(mesh):
    return jax.shard_map(
        on_device,
        mesh=mesh,
        in_specs=(
            P("sym", "row", None),
            P("sym", "row", None),
            P("sym", None, None, None),
            P("sym", "row", None, None),
            P("sym", "row"),
            P("sym", "row"),
            P("sym", "row"),
            P("sym", "row"),
        ),
        out_specs=P("sym", "row", None),
        check_vma=False,
    )
```

```python
import functools

import jax
import jax.numpy as jnp
from jax import lax
from jax.experimental import pallas as pl
from jax.experimental.pallas import tpu as pltpu
from jax.sharding import PartitionSpec as P

F32 = jnp.float32
BF16 = jnp.bfloat16
F16 = jnp.float16
BLOCK = 512
STEP = 1024
NEAR = 8
HALF = 64
PROJ = 2 * HALF
COUP = 96
BODY = PROJ + COUP
SHARE = BODY + 8
COUPLING_SCALE = 32.0
ROWS = ((0,), (0,))
PLAIN = ((1,), (0,))


def split(x):
    high = x.astype(BF16)
    return high, (x - high.astype(F32)).astype(BF16)


def dot(a, b, dims=PLAIN):
    return lax.dot_general(a, b, (dims, ((), ())), preferred_element_type=F32)


def dot3(a, b, dims=PLAIN):
    (ah, al), (bh, bl) = a, b
    return dot(ah, bh, dims) + (dot(ah, bl, dims) + dot(al, bh, dims))


def joined3(a, b, dims=PLAIN):
    (ah, al), (bh, bl) = a, b
    (left,), (right,) = dims
    return dot(
        jnp.concatenate([ah, ah, al], axis=left),
        jnp.concatenate([bh, bl, bh], axis=right),
        dims,
    )


def gram_kernel(start_ref, panel_ref, out_ref, proj, coup):
    step = pl.program_id(0)

    @pl.when(step == 0)
    def _():
        proj[...] = jnp.zeros_like(proj)
        coup[...] = jnp.zeros_like(coup)

    panels = split(panel_ref[0])
    start = split(start_ref[0])
    width = panel_ref.shape[2] // 4

    def columns(*which):
        return tuple(
            jnp.concatenate([p[:, k * width : (k + 1) * width] for k in which], axis=1)
            for p in panels
        )

    proj[...] += dot3(panels, start, ROWS)
    for place, (one, pair) in enumerate(((0, (1, 2)), (1, (2, 3)), (3, (2, 0)))):
        coup[place * width : (place + 1) * width] += dot3(
            columns(one), columns(*pair), ROWS
        )

    @pl.when(step == pl.num_programs(0) - 1)
    def _():
        inner = proj[...]
        top = jnp.max(jnp.abs(inner), axis=(0, 1), keepdims=True)
        exponent = jnp.ceil(jnp.log2(jnp.maximum(top, 1e-30))) - 14.0
        inner = inner * jnp.exp2(-exponent)
        count = out_ref.shape[0]
        out_ref[:, :HALF, :] = inner[:, :128].reshape(count, HALF, 128)
        out_ref[:, HALF:PROJ, :] = inner[:, 128:].reshape(count, HALF, 128)
        lines = jnp.concatenate([coup[:, :width], coup[:, width:]], axis=0)
        lines = lines * COUPLING_SCALE
        out_ref[:, PROJ:BODY, :] = lines.reshape(count, COUP, 128)
        out_ref[:, BODY:, :] = jnp.broadcast_to(
            exponent.reshape(1, 1, 1), (count, 8, 128)
        )


def local_grams(start, panels, count):
    rows, eigen = start.shape[1:]
    columns = panels.shape[2]
    return pl.pallas_call(
        gram_kernel,
        out_shape=jax.ShapeDtypeStruct((count, SHARE, 128), F32),
        grid=(rows // STEP,),
        in_specs=[
            pl.BlockSpec((1, STEP, eigen), lambda i: (0, i, 0)),
            pl.BlockSpec((1, STEP, columns), lambda i: (0, i, 0)),
        ],
        out_specs=pl.BlockSpec((count, SHARE, 128), lambda i: (0, 0, 0)),
        scratch_shapes=[
            pltpu.VMEM((columns, eigen), F32),
            pltpu.VMEM((3 * columns // 4, columns // 2), F32),
        ],
        compiler_params=pltpu.CompilerParams(vmem_limit_bytes=40 << 20),
        cost_estimate=pl.CostEstimate(
            flops=6 * rows * columns * (eigen + columns // 2),
            bytes_accessed=4 * rows * (eigen + columns),
            transcendentals=0,
        ),
        name="grams",
    )(start, panels)


def fetch_kernel(which_ref, start_ref, panel_ref, start_out, high_out, low_out):
    high, low = split(panel_ref[0])
    start_out[0] = start_ref[0]
    high_out[0] = high
    low_out[0] = low


def fetched_blocks(which, start, panels):
    count = which.shape[0]
    eigen, columns = start.shape[2], panels.shape[2]

    def named(width):
        return pl.BlockSpec((1, BLOCK, width), lambda t, which: (0, which[t], 0))

    def kept(width):
        return pl.BlockSpec((1, BLOCK, width), lambda t, which: (t, 0, 0))

    return pl.pallas_call(
        fetch_kernel,
        out_shape=(
            jax.ShapeDtypeStruct((count, BLOCK, eigen), F32),
            jax.ShapeDtypeStruct((count, BLOCK, columns), BF16),
            jax.ShapeDtypeStruct((count, BLOCK, columns), BF16),
        ),
        grid_spec=pltpu.PrefetchScalarGridSpec(
            num_scalar_prefetch=1,
            grid=(count,),
            in_specs=[named(eigen), named(columns)],
            out_specs=(kept(eigen), kept(columns), kept(columns)),
        ),
        compiler_params=pltpu.CompilerParams(vmem_limit_bytes=10 << 20),
        cost_estimate=pl.CostEstimate(
            flops=count * BLOCK * columns,
            bytes_accessed=8 * count * BLOCK * (columns + eigen),
            transcendentals=0,
        ),
        name="fetch",
    )(which, start, panels)


def updated_block(start, panels, upper, lower, limits):
    high, low = panels
    back = start - (dot(high, upper) + (dot(high, lower) + dot(low, upper)))
    line = lax.broadcasted_iota(jnp.int32, (BLOCK, back.shape[1]), 0)
    live = jnp.concatenate([line < limit for limit in limits], axis=0)
    return jnp.where(live, back, 0.0).astype(BF16)


def solve_kernel(
    want_ref,
    limit_ref,
    sums_ref,
    exponent_ref,
    factor_ref,
    start_ref,
    high_ref,
    low_ref,
    out_ref,
    upper,
    lower,
):
    count = sums_ref.shape[0]
    width = factor_ref.shape[2]
    scale = jnp.exp2(exponent_ref[:1, :])
    size = (count * HALF, 128)
    inner = split(
        jnp.concatenate(
            [
                sums_ref[:, :HALF, :].reshape(size) * scale,
                sums_ref[:, HALF:PROJ, :].reshape(size) * scale,
            ],
            axis=1,
        )
    )
    links = split(sums_ref[:, PROJ:BODY, :].reshape(count * COUP, 128))

    def part(pair, k):
        return tuple(p[k * width : (k + 1) * width] for p in pair)

    factors = [split(factor_ref[0, level]) for level in range(4)]
    current = [joined3(factors[level], part(inner, level)) for level in range(4)]
    turned = ((1,), (1,))
    places = {
        3: ((0, 5, turned), (1, 4, PLAIN), (2, 2, turned)),
        2: ((0, 3, PLAIN), (1, 1, PLAIN)),
        1: ((0, 0, PLAIN),),
    }
    chained = {}
    for later, entries in places.items():
        products = [joined3(factors[k], part(links, at), dims) for k, at, dims in entries]
        chained[later] = split(jnp.concatenate(products, axis=0))
    parts = [None] * 4
    for level in (3, 2, 1, 0):
        parts[level] = split(current[level])
        if level:
            moved = joined3(chained[level], parts[level])
            for k in range(level):
                current[k] = current[k] - moved[k * width : (k + 1) * width]
    upper[...] = jnp.concatenate([p[0] for p in parts], axis=0)
    lower[...] = jnp.concatenate([p[1] for p in parts], axis=0)
    shape = out_ref.shape
    limits = [limit_ref[want_ref[t]] for t in range(shape[0])]
    tall = (shape[0] * shape[1], -1)
    out_ref[...] = updated_block(
        start_ref[...].reshape(tall),
        (high_ref[...].reshape(tall), low_ref[...].reshape(tall)),
        upper[...],
        lower[...],
        limits,
    ).reshape(shape)


def left_kernel(
    left_ref,
    occupied_ref,
    limit_ref,
    upper,
    lower,
    start_ref,
    panel_ref,
    tile_ref,
    high_out,
    low_out,
):
    turn = pl.program_id(0)
    block = updated_block(
        start_ref[0],
        split(panel_ref[0]),
        upper[...],
        lower[...],
        [limit_ref[left_ref[turn]] * occupied_ref[turn]],
    )
    high_out[...], low_out[...] = split(dot(block, tile_ref[0, 0], ROWS))


SCALARS = pl.BlockSpec(memory_space=pltpu.SMEM)
ARRAY = pl.BlockSpec(memory_space=pltpu.VMEM)


def update_cost(blocks, columns, eigen):
    return pl.CostEstimate(
        flops=6 * blocks * BLOCK * columns * eigen,
        bytes_accessed=4 * blocks * BLOCK * (columns + eigen),
        transcendentals=0,
    )


def solve_and_update(want, limits, sums, exponent, factors, start, high, low):
    count = want.shape[0]
    eigen, columns = start.shape[2], high.shape[2]
    coefficients = jax.ShapeDtypeStruct((columns, eigen), BF16)
    return pl.pallas_call(
        solve_kernel,
        out_shape=(
            jax.ShapeDtypeStruct((count, BLOCK, eigen), BF16),
            coefficients,
            coefficients,
        ),
        in_specs=[SCALARS] * 2 + [ARRAY] * 6,
        out_specs=(ARRAY,) * 3,
        compiler_params=pltpu.CompilerParams(vmem_limit_bytes=12 << 20),
        cost_estimate=update_cost(count, columns, eigen),
        name="solve",
    )(want, limits, sums, exponent, factors, start, high, low)


def left_products(left, occupied, limits, upper, lower, start, panels, tiles):
    count = left.shape[0]
    eigen, columns = start.shape[2], panels.shape[2]

    def named(width):
        return pl.BlockSpec((1, BLOCK, width), lambda t, which, *_: (0, which[t], 0))

    def whole(shape):
        return pl.BlockSpec(shape, lambda t, *_: (0, 0))

    wide = pl.BlockSpec((eigen, BLOCK), lambda t, *_: (0, t))
    return pl.pallas_call(
        left_kernel,
        out_shape=(jax.ShapeDtypeStruct((eigen, count * BLOCK), BF16),) * 2,
        grid_spec=pltpu.PrefetchScalarGridSpec(
            num_scalar_prefetch=3,
            grid=(count,),
            in_specs=[
                whole((columns, eigen)),
                whole((columns, eigen)),
                named(eigen),
                named(columns),
                pl.BlockSpec((1, 1, BLOCK, BLOCK), lambda t, *_: (0, t, 0, 0)),
            ],
            out_specs=(wide, wide),
        ),
        compiler_params=pltpu.CompilerParams(vmem_limit_bytes=16 << 20),
        cost_estimate=update_cost(count, columns, eigen),
        name="left",
    )(left, occupied, limits, upper, lower, start, panels, tiles)


def dipole_kernel(high_ref, low_ref, right_ref, out_ref):
    right = right_ref[...].reshape(-1, right_ref.shape[2])
    out_ref[...] = (dot(high_ref[...], right) + dot(low_ref[...], right)).astype(BF16)


def tile_products(high, low, right):
    eigen = right.shape[2]
    return pl.pallas_call(
        dipole_kernel,
        out_shape=jax.ShapeDtypeStruct((eigen, eigen), BF16),
        in_specs=[ARRAY] * 3,
        out_specs=ARRAY,
        compiler_params=pltpu.CompilerParams(vmem_limit_bytes=8 << 20),
        name="dipole",
    )(high, low, right)


def passed_along(block, axis, distance):
    devices = range(lax.axis_size(axis))
    route = [((i - distance) % len(devices), i) for i in devices]
    return lax.ppermute(block, axis, route)


def exchanged(shares, groups=None):
    return lax.all_to_all(shares, "row", 0, 0, axis_index_groups=groups, tiled=True)


def combined(shares):
    shares = [share.astype(F32) for share in shares]
    exponents = [share[BODY:] for share in shares]
    exponent = functools.reduce(jnp.maximum, exponents)
    exponent = exponent + float(len(shares).bit_length() - 1)
    proj = sum(
        share[:PROJ] * jnp.exp2(own[:1] - exponent[:1])
        for share, own in zip(shares, exponents)
    )
    coup = sum(share[PROJ:BODY] for share in shares) * (1.0 / len(shares))
    return jnp.concatenate([proj, coup], axis=0), exponent


def around(share, step):
    count = lax.axis_size("row")
    route = [((i + step) % count, i) for i in range(count)]
    return lax.ppermute(share, "row", route)


def on_device(
    vectors, reflectors, factors, tiles, tile_left, tile_right, tile_occupied_mask, channels
):
    count = lax.axis_size("row")
    vectors = pltpu.with_memory_space_constraint(vectors, pltpu.HBM)
    reflectors = pltpu.with_memory_space_constraint(reflectors, pltpu.HBM)
    want = passed_along(tile_right[0], "sym", 1)
    far = count // NEAR
    inside = [[far_at * NEAR + at for at in range(NEAR)] for far_at in range(far)]
    shares = local_grams(vectors, reflectors, NEAR).astype(F16)
    want, shares = lax.optimization_barrier((want, shares))
    terms = exchanged(shares, inside)
    owned = jnp.concatenate(combined([terms[at] for at in range(NEAR)]), axis=0)
    owned = owned.astype(F16)
    want, owned = lax.optimization_barrier((want, owned))
    named = fetched_blocks(want, vectors, reflectors)
    others = [around(owned, NEAR * step) for step in (1, far - 1, *range(2, far - 1))]
    others, named = lax.optimization_barrier((others, named))
    body, exponent = combined([owned, *others])
    copies = jnp.broadcast_to(body.astype(F16), (NEAR, BODY, 128))
    sums = exchanged(copies, inside).astype(F32)
    packed, upper, lower = solve_and_update(
        want, channels[0], sums, exponent, factors, *named
    )
    right = passed_along(packed, "sym", -1)
    left = left_products(
        tile_left[0],
        tile_occupied_mask[0],
        channels[0],
        upper,
        lower,
        vectors,
        reflectors,
        tiles,
    )
    partial = tile_products(*left, right)
    eigen = partial.shape[1]
    owned = exchanged(partial.reshape(count, eigen // count, eigen))
    return jnp.sum(owned.astype(F32), axis=0)[None]


def solution(mesh):
    return jax.shard_map(
        on_device,
        mesh=mesh,
        in_specs=(
            P("sym", "row", None),
            P("sym", "row", None),
            P("sym", None, None, None),
            P("sym", "row", None, None),
            P("sym", "row"),
            P("sym", "row"),
            P("sym", "row"),
            P("sym", "row"),
        ),
        out_specs=P("sym", "row", None),
        check_vma=False,
    )
```

```python
import functools

import jax
import jax.numpy as jnp
from jax import lax
from jax.experimental import pallas as pl
from jax.experimental.pallas import tpu as pltpu
from jax.sharding import PartitionSpec as P

F32 = jnp.float32
BF16 = jnp.bfloat16
F16 = jnp.float16
BLOCK = 512
STEP = 1024
NEAR = 8
HALF = 64
PROJ = 2 * HALF
COUP = 96
BODY = PROJ + COUP
SHARE = BODY + 8
COUPLING_SCALE = 32.0
ROWS = ((0,), (0,))
PLAIN = ((1,), (0,))


def split(x):
    high = x.astype(BF16)
    return high, (x - high.astype(F32)).astype(BF16)


def dot(a, b, dims=PLAIN):
    return lax.dot_general(a, b, (dims, ((), ())), preferred_element_type=F32)


def dot3(a, b, dims=PLAIN):
    (ah, al), (bh, bl) = a, b
    return dot(ah, bh, dims) + (dot(ah, bl, dims) + dot(al, bh, dims))


def joined3(a, b, dims=PLAIN):
    (ah, al), (bh, bl) = a, b
    (left,), (right,) = dims
    return dot(
        jnp.concatenate([ah, ah, al], axis=left),
        jnp.concatenate([bh, bl, bh], axis=right),
        dims,
    )


def gram_kernel(start_ref, panel_ref, out_ref, proj, coup):
    step = pl.program_id(0)

    @pl.when(step == 0)
    def _():
        proj[...] = jnp.zeros_like(proj)
        coup[...] = jnp.zeros_like(coup)

    panels = split(panel_ref[0])
    start = split(start_ref[0])
    width = panel_ref.shape[2] // 4

    def columns(*which):
        return tuple(
            jnp.concatenate([p[:, k * width : (k + 1) * width] for k in which], axis=1)
            for p in panels
        )

    proj[...] += dot3(panels, start, ROWS)
    for place, (one, pair) in enumerate(((0, (1, 2)), (1, (2, 3)), (3, (2, 0)))):
        coup[place * width : (place + 1) * width] += dot3(
            columns(one), columns(*pair), ROWS
        )

    @pl.when(step == pl.num_programs(0) - 1)
    def _():
        inner = proj[...]
        top = jnp.max(jnp.abs(inner), axis=(0, 1), keepdims=True)
        exponent = jnp.ceil(jnp.log2(jnp.maximum(top, 1e-30))) - 14.0
        inner = inner * jnp.exp2(-exponent)
        count = out_ref.shape[0]
        out_ref[:, :HALF, :] = inner[:, :128].reshape(count, HALF, 128)
        out_ref[:, HALF:PROJ, :] = inner[:, 128:].reshape(count, HALF, 128)
        lines = jnp.concatenate([coup[:, :width], coup[:, width:]], axis=0)
        lines = lines * COUPLING_SCALE
        out_ref[:, PROJ:BODY, :] = lines.reshape(count, COUP, 128)
        out_ref[:, BODY:, :] = jnp.broadcast_to(
            exponent.reshape(1, 1, 1), (count, 8, 128)
        )


def local_grams(start, panels, count):
    rows, eigen = start.shape[1:]
    columns = panels.shape[2]
    return pl.pallas_call(
        gram_kernel,
        out_shape=jax.ShapeDtypeStruct((count, SHARE, 128), F32),
        grid=(rows // STEP,),
        in_specs=[
            pl.BlockSpec((1, STEP, eigen), lambda i: (0, i, 0)),
            pl.BlockSpec((1, STEP, columns), lambda i: (0, i, 0)),
        ],
        out_specs=pl.BlockSpec((count, SHARE, 128), lambda i: (0, 0, 0)),
        scratch_shapes=[
            pltpu.VMEM((columns, eigen), F32),
            pltpu.VMEM((3 * columns // 4, columns // 2), F32),
        ],
        compiler_params=pltpu.CompilerParams(vmem_limit_bytes=40 << 20),
        cost_estimate=pl.CostEstimate(
            flops=6 * rows * columns * (eigen + columns // 2),
            bytes_accessed=4 * rows * (eigen + columns),
            transcendentals=0,
        ),
        name="grams",
    )(start, panels)


def fetch_kernel(which_ref, start_ref, panel_ref, start_out, high_out, low_out):
    high, low = split(panel_ref[0])
    start_out[0] = start_ref[0]
    high_out[0] = high
    low_out[0] = low


def fetched_blocks(which, start, panels):
    count = which.shape[0]
    eigen, columns = start.shape[2], panels.shape[2]

    def named(width):
        return pl.BlockSpec((1, BLOCK, width), lambda t, which: (0, which[t], 0))

    def kept(width):
        return pl.BlockSpec((1, BLOCK, width), lambda t, which: (t, 0, 0))

    return pl.pallas_call(
        fetch_kernel,
        out_shape=(
            jax.ShapeDtypeStruct((count, BLOCK, eigen), F32),
            jax.ShapeDtypeStruct((count, BLOCK, columns), BF16),
            jax.ShapeDtypeStruct((count, BLOCK, columns), BF16),
        ),
        grid_spec=pltpu.PrefetchScalarGridSpec(
            num_scalar_prefetch=1,
            grid=(count,),
            in_specs=[named(eigen), named(columns)],
            out_specs=(kept(eigen), kept(columns), kept(columns)),
        ),
        compiler_params=pltpu.CompilerParams(vmem_limit_bytes=10 << 20),
        cost_estimate=pl.CostEstimate(
            flops=count * BLOCK * columns,
            bytes_accessed=8 * count * BLOCK * (columns + eigen),
            transcendentals=0,
        ),
        name="fetch",
    )(which, start, panels)


def updated_block(start, panels, upper, lower, limits):
    high, low = panels
    back = start - (dot(high, upper) + (dot(high, lower) + dot(low, upper)))
    line = lax.broadcasted_iota(jnp.int32, (BLOCK, back.shape[1]), 0)
    live = jnp.concatenate([line < limit for limit in limits], axis=0)
    return jnp.where(live, back, 0.0).astype(BF16)


def solve_kernel(
    want_ref,
    limit_ref,
    sums_ref,
    exponent_ref,
    factor_ref,
    start_ref,
    high_ref,
    low_ref,
    out_ref,
    upper,
    lower,
):
    count = sums_ref.shape[0]
    width = factor_ref.shape[2]
    scale = jnp.exp2(exponent_ref[:1, :])
    size = (count * HALF, 128)
    inner = split(
        jnp.concatenate(
            [
                sums_ref[:, :HALF, :].reshape(size) * scale,
                sums_ref[:, HALF:PROJ, :].reshape(size) * scale,
            ],
            axis=1,
        )
    )
    links = split(sums_ref[:, PROJ:BODY, :].reshape(count * COUP, 128))

    def part(pair, k):
        return tuple(p[k * width : (k + 1) * width] for p in pair)

    factors = [split(factor_ref[0, level]) for level in range(4)]
    current = [joined3(factors[level], part(inner, level)) for level in range(4)]
    turned = ((1,), (1,))

    def both(k, one, other):
        wide = tuple(
            jnp.concatenate(pair, axis=1) for pair in zip(part(links, one), part(links, other))
        )
        product = joined3(factors[k], wide)
        return product[:, :width], product[:, width:]

    to_01, to_02 = both(0, 0, 3)
    to_12, to_13 = both(1, 1, 4)
    to_23 = joined3(factors[2], part(links, 2), turned)
    to_03 = joined3(factors[0], part(links, 5), turned)
    chained = {
        3: split(jnp.concatenate([to_03, to_13, to_23], axis=0)),
        2: split(jnp.concatenate([to_02, to_12], axis=0)),
        1: split(to_01),
    }
    parts = [None] * 4
    for level in (3, 2, 1, 0):
        parts[level] = split(current[level])
        if level:
            moved = joined3(chained[level], parts[level])
            for k in range(level):
                current[k] = current[k] - moved[k * width : (k + 1) * width]
    upper[...] = jnp.concatenate([p[0] for p in parts], axis=0)
    lower[...] = jnp.concatenate([p[1] for p in parts], axis=0)
    shape = out_ref.shape
    limits = [limit_ref[want_ref[t]] for t in range(shape[0])]
    tall = (shape[0] * shape[1], -1)
    out_ref[...] = updated_block(
        start_ref[...].reshape(tall),
        (high_ref[...].reshape(tall), low_ref[...].reshape(tall)),
        upper[...],
        lower[...],
        limits,
    ).reshape(shape)


def left_kernel(
    left_ref,
    occupied_ref,
    limit_ref,
    upper,
    lower,
    start_ref,
    panel_ref,
    tile_ref,
    high_out,
    low_out,
):
    turn = pl.program_id(0)
    block = updated_block(
        start_ref[0],
        split(panel_ref[0]),
        upper[...],
        lower[...],
        [limit_ref[left_ref[turn]] * occupied_ref[turn]],
    )
    high_out[...], low_out[...] = split(dot(block, tile_ref[0, 0], ROWS))


SCALARS = pl.BlockSpec(memory_space=pltpu.SMEM)
ARRAY = pl.BlockSpec(memory_space=pltpu.VMEM)


def update_cost(blocks, columns, eigen):
    return pl.CostEstimate(
        flops=6 * blocks * BLOCK * columns * eigen,
        bytes_accessed=4 * blocks * BLOCK * (columns + eigen),
        transcendentals=0,
    )


def solve_and_update(want, limits, sums, exponent, factors, start, high, low):
    count = want.shape[0]
    eigen, columns = start.shape[2], high.shape[2]
    coefficients = jax.ShapeDtypeStruct((columns, eigen), BF16)
    return pl.pallas_call(
        solve_kernel,
        out_shape=(
            jax.ShapeDtypeStruct((count, BLOCK, eigen), BF16),
            coefficients,
            coefficients,
        ),
        in_specs=[SCALARS] * 2 + [ARRAY] * 6,
        out_specs=(ARRAY,) * 3,
        compiler_params=pltpu.CompilerParams(vmem_limit_bytes=12 << 20),
        cost_estimate=update_cost(count, columns, eigen),
        name="solve",
    )(want, limits, sums, exponent, factors, start, high, low)


def left_products(left, occupied, limits, upper, lower, start, panels, tiles):
    count = left.shape[0]
    eigen, columns = start.shape[2], panels.shape[2]

    def named(width):
        return pl.BlockSpec((1, BLOCK, width), lambda t, which, *_: (0, which[t], 0))

    def whole(shape):
        return pl.BlockSpec(shape, lambda t, *_: (0, 0))

    wide = pl.BlockSpec((eigen, BLOCK), lambda t, *_: (0, t))
    return pl.pallas_call(
        left_kernel,
        out_shape=(jax.ShapeDtypeStruct((eigen, count * BLOCK), BF16),) * 2,
        grid_spec=pltpu.PrefetchScalarGridSpec(
            num_scalar_prefetch=3,
            grid=(count,),
            in_specs=[
                whole((columns, eigen)),
                whole((columns, eigen)),
                named(eigen),
                named(columns),
                pl.BlockSpec((1, 1, BLOCK, BLOCK), lambda t, *_: (0, t, 0, 0)),
            ],
            out_specs=(wide, wide),
        ),
        compiler_params=pltpu.CompilerParams(vmem_limit_bytes=16 << 20),
        cost_estimate=update_cost(count, columns, eigen),
        name="left",
    )(left, occupied, limits, upper, lower, start, panels, tiles)


def dipole_kernel(high_ref, low_ref, right_ref, out_ref):
    right = right_ref[...].reshape(-1, right_ref.shape[2])
    out_ref[...] = (dot(high_ref[...], right) + dot(low_ref[...], right)).astype(BF16)


def tile_products(high, low, right):
    eigen = right.shape[2]
    return pl.pallas_call(
        dipole_kernel,
        out_shape=jax.ShapeDtypeStruct((eigen, eigen), BF16),
        in_specs=[ARRAY] * 3,
        out_specs=ARRAY,
        compiler_params=pltpu.CompilerParams(vmem_limit_bytes=8 << 20),
        name="dipole",
    )(high, low, right)


def passed_along(block, axis, distance):
    devices = range(lax.axis_size(axis))
    route = [((i - distance) % len(devices), i) for i in devices]
    return lax.ppermute(block, axis, route)


def exchanged(shares, groups=None):
    return lax.all_to_all(shares, "row", 0, 0, axis_index_groups=groups, tiled=True)


def combined(shares):
    shares = [share.astype(F32) for share in shares]
    exponents = [share[BODY:] for share in shares]
    exponent = functools.reduce(jnp.maximum, exponents)
    exponent = exponent + float(len(shares).bit_length() - 1)
    proj = sum(
        share[:PROJ] * jnp.exp2(own[:1] - exponent[:1])
        for share, own in zip(shares, exponents)
    )
    coup = sum(share[PROJ:BODY] for share in shares) * (1.0 / len(shares))
    return jnp.concatenate([proj, coup], axis=0), exponent


def around(share, step):
    count = lax.axis_size("row")
    route = [((i + step) % count, i) for i in range(count)]
    return lax.ppermute(share, "row", route)


def on_device(
    vectors, reflectors, factors, tiles, tile_left, tile_right, tile_occupied_mask, channels
):
    count = lax.axis_size("row")
    vectors = pltpu.with_memory_space_constraint(vectors, pltpu.HBM)
    reflectors = pltpu.with_memory_space_constraint(reflectors, pltpu.HBM)
    want = passed_along(tile_right[0], "sym", 1)
    far = count // NEAR
    inside = [[far_at * NEAR + at for at in range(NEAR)] for far_at in range(far)]
    shares = local_grams(vectors, reflectors, NEAR).astype(F16)
    want, shares = lax.optimization_barrier((want, shares))
    terms = exchanged(shares, inside)
    owned = jnp.concatenate(combined([terms[at] for at in range(NEAR)]), axis=0)
    owned = owned.astype(F16)
    want, owned = lax.optimization_barrier((want, owned))
    named = fetched_blocks(want, vectors, reflectors)
    others = [around(owned, NEAR * step) for step in (1, far - 1, *range(2, far - 1))]
    others, named = lax.optimization_barrier((others, named))
    body, exponent = combined([owned, *others])
    copies = jnp.broadcast_to(body.astype(F16), (NEAR, BODY, 128))
    sums = exchanged(copies, inside).astype(F32)
    packed, upper, lower = solve_and_update(
        want, channels[0], sums, exponent, factors, *named
    )
    right = passed_along(packed, "sym", -1)
    left = left_products(
        tile_left[0],
        tile_occupied_mask[0],
        channels[0],
        upper,
        lower,
        vectors,
        reflectors,
        tiles,
    )
    partial = tile_products(*left, right)
    eigen = partial.shape[1]
    owned = exchanged(partial.reshape(count, eigen // count, eigen))
    return jnp.sum(owned.astype(F32), axis=0)[None]


def solution(mesh):
    return jax.shard_map(
        on_device,
        mesh=mesh,
        in_specs=(
            P("sym", "row", None),
            P("sym", "row", None),
            P("sym", None, None, None),
            P("sym", "row", None, None),
            P("sym", "row"),
            P("sym", "row"),
            P("sym", "row"),
            P("sym", "row"),
        ),
        out_specs=P("sym", "row", None),
        check_vma=False,
    )
```

```python
import functools

import jax
import jax.numpy as jnp
from jax import lax
from jax.experimental import pallas as pl
from jax.experimental.pallas import tpu as pltpu
from jax.sharding import PartitionSpec as P

F32 = jnp.float32
BF16 = jnp.bfloat16
F16 = jnp.float16
BLOCK = 512
STEP = 1024
NEAR = 8
HALF = 64
PROJ = 2 * HALF
COUP = 96
BODY = PROJ + COUP
SHARE = BODY + 8
COUPLING_SCALE = 32.0
ROWS = ((0,), (0,))
PLAIN = ((1,), (0,))


def split(x):
    high = x.astype(BF16)
    return high, (x - high.astype(F32)).astype(BF16)


def dot(a, b, dims=PLAIN):
    return lax.dot_general(a, b, (dims, ((), ())), preferred_element_type=F32)


def dot3(a, b, dims=PLAIN):
    (ah, al), (bh, bl) = a, b
    return dot(ah, bh, dims) + (dot(ah, bl, dims) + dot(al, bh, dims))


def joined3(a, b, dims=PLAIN):
    (ah, al), (bh, bl) = a, b
    (left,), (right,) = dims
    return dot(
        jnp.concatenate([ah, ah, al], axis=left),
        jnp.concatenate([bh, bl, bh], axis=right),
        dims,
    )


def gram_kernel(start_ref, panel_ref, out_ref, proj, coup):
    step = pl.program_id(0)

    @pl.when(step == 0)
    def _():
        proj[...] = jnp.zeros_like(proj)
        coup[...] = jnp.zeros_like(coup)

    panels = split(panel_ref[0])
    start = split(start_ref[0])
    width = panel_ref.shape[2] // 4

    def columns(*which):
        return tuple(
            jnp.concatenate([p[:, k * width : (k + 1) * width] for k in which], axis=1)
            for p in panels
        )

    proj[...] += dot3(panels, start, ROWS)
    for place, (one, pair) in enumerate(((0, (1, 2)), (1, (2, 3)), (3, (2, 0)))):
        coup[place * width : (place + 1) * width] += dot3(
            columns(one), columns(*pair), ROWS
        )

    @pl.when(step == pl.num_programs(0) - 1)
    def _():
        inner = proj[...]
        top = jnp.max(jnp.abs(inner), axis=(0, 1), keepdims=True)
        exponent = jnp.ceil(jnp.log2(jnp.maximum(top, 1e-30))) - 14.0
        inner = inner * jnp.exp2(-exponent)
        count = out_ref.shape[0]
        out_ref[:, :HALF, :] = inner[:, :128].reshape(count, HALF, 128)
        out_ref[:, HALF:PROJ, :] = inner[:, 128:].reshape(count, HALF, 128)
        lines = jnp.concatenate([coup[:, :width], coup[:, width:]], axis=0)
        lines = lines * COUPLING_SCALE
        out_ref[:, PROJ:BODY, :] = lines.reshape(count, COUP, 128)
        out_ref[:, BODY:, :] = jnp.broadcast_to(
            exponent.reshape(1, 1, 1), (count, 8, 128)
        )


def local_grams(start, panels, count):
    rows, eigen = start.shape[1:]
    columns = panels.shape[2]
    return pl.pallas_call(
        gram_kernel,
        out_shape=jax.ShapeDtypeStruct((count, SHARE, 128), F32),
        grid=(rows // STEP,),
        in_specs=[
            pl.BlockSpec((1, STEP, eigen), lambda i: (0, i, 0)),
            pl.BlockSpec((1, STEP, columns), lambda i: (0, i, 0)),
        ],
        out_specs=pl.BlockSpec((count, SHARE, 128), lambda i: (0, 0, 0)),
        scratch_shapes=[
            pltpu.VMEM((columns, eigen), F32),
            pltpu.VMEM((3 * columns // 4, columns // 2), F32),
        ],
        compiler_params=pltpu.CompilerParams(vmem_limit_bytes=40 << 20),
        cost_estimate=pl.CostEstimate(
            flops=6 * rows * columns * (eigen + columns // 2),
            bytes_accessed=4 * rows * (eigen + columns),
            transcendentals=0,
        ),
        name="grams",
    )(start, panels)


def fetch_kernel(which_ref, start_ref, panel_ref, start_out, high_out, low_out):
    high, low = split(panel_ref[0])
    start_out[0] = start_ref[0]
    high_out[0] = high
    low_out[0] = low


def fetched_blocks(which, start, panels):
    count = which.shape[0]
    eigen, columns = start.shape[2], panels.shape[2]

    def named(width):
        return pl.BlockSpec((1, BLOCK, width), lambda t, which: (0, which[t], 0))

    def kept(width):
        return pl.BlockSpec((1, BLOCK, width), lambda t, which: (t, 0, 0))

    return pl.pallas_call(
        fetch_kernel,
        out_shape=(
            jax.ShapeDtypeStruct((count, BLOCK, eigen), F32),
            jax.ShapeDtypeStruct((count, BLOCK, columns), BF16),
            jax.ShapeDtypeStruct((count, BLOCK, columns), BF16),
        ),
        grid_spec=pltpu.PrefetchScalarGridSpec(
            num_scalar_prefetch=1,
            grid=(count,),
            in_specs=[named(eigen), named(columns)],
            out_specs=(kept(eigen), kept(columns), kept(columns)),
        ),
        compiler_params=pltpu.CompilerParams(vmem_limit_bytes=10 << 20),
        cost_estimate=pl.CostEstimate(
            flops=count * BLOCK * columns,
            bytes_accessed=8 * count * BLOCK * (columns + eigen),
            transcendentals=0,
        ),
        name="fetch",
    )(which, start, panels)


def updated_block(start, panels, upper, lower, limits):
    back = start - joined3(panels, (upper, lower))
    line = lax.broadcasted_iota(jnp.int32, (BLOCK, back.shape[1]), 0)
    live = jnp.concatenate([line < limit for limit in limits], axis=0)
    return jnp.where(live, back, 0.0).astype(BF16)


def solve_kernel(
    want_ref,
    limit_ref,
    sums_ref,
    exponent_ref,
    factor_ref,
    start_ref,
    high_ref,
    low_ref,
    out_ref,
    upper,
    lower,
):
    count = sums_ref.shape[0]
    width = factor_ref.shape[2]
    scale = jnp.exp2(exponent_ref[:1, :])
    size = (count * HALF, 128)
    inner = split(
        jnp.concatenate(
            [
                sums_ref[:, :HALF, :].reshape(size) * scale,
                sums_ref[:, HALF:PROJ, :].reshape(size) * scale,
            ],
            axis=1,
        )
    )
    links = split(sums_ref[:, PROJ:BODY, :].reshape(count * COUP, 128))

    def part(pair, k):
        return tuple(p[k * width : (k + 1) * width] for p in pair)

    factors = [split(factor_ref[0, level]) for level in range(4)]
    current = [joined3(factors[level], part(inner, level)) for level in range(4)]
    turned = ((1,), (1,))
    places = {
        3: ((0, 5, turned), (1, 4, PLAIN), (2, 2, turned)),
        2: ((0, 3, PLAIN), (1, 1, PLAIN)),
        1: ((0, 0, PLAIN),),
    }
    chained = {}
    for later, entries in places.items():
        products = [joined3(factors[k], part(links, at), dims) for k, at, dims in entries]
        chained[later] = split(jnp.concatenate(products, axis=0))
    parts = [None] * 4
    for level in (3, 2, 1, 0):
        parts[level] = split(current[level])
        if level:
            moved = joined3(chained[level], parts[level])
            for k in range(level):
                current[k] = current[k] - moved[k * width : (k + 1) * width]
    upper[...] = jnp.concatenate([p[0] for p in parts], axis=0)
    lower[...] = jnp.concatenate([p[1] for p in parts], axis=0)
    shape = out_ref.shape
    limits = [limit_ref[want_ref[t]] for t in range(shape[0])]
    tall = (shape[0] * shape[1], -1)
    out_ref[...] = updated_block(
        start_ref[...].reshape(tall),
        (high_ref[...].reshape(tall), low_ref[...].reshape(tall)),
        upper[...],
        lower[...],
        limits,
    ).reshape(shape)


def left_kernel(
    left_ref,
    occupied_ref,
    limit_ref,
    upper,
    lower,
    start_ref,
    panel_ref,
    tile_ref,
    high_out,
    low_out,
):
    turn = pl.program_id(0)
    block = updated_block(
        start_ref[0],
        split(panel_ref[0]),
        upper[...],
        lower[...],
        [limit_ref[left_ref[turn]] * occupied_ref[turn]],
    )
    high_out[...], low_out[...] = split(dot(block, tile_ref[0, 0], ROWS))


SCALARS = pl.BlockSpec(memory_space=pltpu.SMEM)
ARRAY = pl.BlockSpec(memory_space=pltpu.VMEM)


def update_cost(blocks, columns, eigen):
    return pl.CostEstimate(
        flops=6 * blocks * BLOCK * columns * eigen,
        bytes_accessed=4 * blocks * BLOCK * (columns + eigen),
        transcendentals=0,
    )


def solve_and_update(want, limits, sums, exponent, factors, start, high, low):
    count = want.shape[0]
    eigen, columns = start.shape[2], high.shape[2]
    coefficients = jax.ShapeDtypeStruct((columns, eigen), BF16)
    return pl.pallas_call(
        solve_kernel,
        out_shape=(
            jax.ShapeDtypeStruct((count, BLOCK, eigen), BF16),
            coefficients,
            coefficients,
        ),
        in_specs=[SCALARS] * 2 + [ARRAY] * 6,
        out_specs=(ARRAY,) * 3,
        compiler_params=pltpu.CompilerParams(vmem_limit_bytes=12 << 20),
        cost_estimate=update_cost(count, columns, eigen),
        name="solve",
    )(want, limits, sums, exponent, factors, start, high, low)


def left_products(left, occupied, limits, upper, lower, start, panels, tiles):
    count = left.shape[0]
    eigen, columns = start.shape[2], panels.shape[2]

    def named(width):
        return pl.BlockSpec((1, BLOCK, width), lambda t, which, *_: (0, which[t], 0))

    def whole(shape):
        return pl.BlockSpec(shape, lambda t, *_: (0, 0))

    wide = pl.BlockSpec((eigen, BLOCK), lambda t, *_: (0, t))
    return pl.pallas_call(
        left_kernel,
        out_shape=(jax.ShapeDtypeStruct((eigen, count * BLOCK), BF16),) * 2,
        grid_spec=pltpu.PrefetchScalarGridSpec(
            num_scalar_prefetch=3,
            grid=(count,),
            in_specs=[
                whole((columns, eigen)),
                whole((columns, eigen)),
                named(eigen),
                named(columns),
                pl.BlockSpec((1, 1, BLOCK, BLOCK), lambda t, *_: (0, t, 0, 0)),
            ],
            out_specs=(wide, wide),
        ),
        compiler_params=pltpu.CompilerParams(vmem_limit_bytes=16 << 20),
        cost_estimate=update_cost(count, columns, eigen),
        name="left",
    )(left, occupied, limits, upper, lower, start, panels, tiles)


def dipole_kernel(high_ref, low_ref, right_ref, out_ref):
    right = right_ref[...].reshape(-1, right_ref.shape[2])
    out_ref[...] = (dot(high_ref[...], right) + dot(low_ref[...], right)).astype(BF16)


def tile_products(high, low, right):
    eigen = right.shape[2]
    return pl.pallas_call(
        dipole_kernel,
        out_shape=jax.ShapeDtypeStruct((eigen, eigen), BF16),
        in_specs=[ARRAY] * 3,
        out_specs=ARRAY,
        compiler_params=pltpu.CompilerParams(vmem_limit_bytes=8 << 20),
        name="dipole",
    )(high, low, right)


def passed_along(block, axis, distance):
    devices = range(lax.axis_size(axis))
    route = [((i - distance) % len(devices), i) for i in devices]
    return lax.ppermute(block, axis, route)


def exchanged(shares, groups=None):
    return lax.all_to_all(shares, "row", 0, 0, axis_index_groups=groups, tiled=True)


def combined(shares):
    shares = [share.astype(F32) for share in shares]
    exponents = [share[BODY:] for share in shares]
    exponent = functools.reduce(jnp.maximum, exponents)
    exponent = exponent + float(len(shares).bit_length() - 1)
    proj = sum(
        share[:PROJ] * jnp.exp2(own[:1] - exponent[:1])
        for share, own in zip(shares, exponents)
    )
    coup = sum(share[PROJ:BODY] for share in shares) * (1.0 / len(shares))
    return jnp.concatenate([proj, coup], axis=0), exponent


def around(share, step):
    count = lax.axis_size("row")
    route = [((i + step) % count, i) for i in range(count)]
    return lax.ppermute(share, "row", route)


def on_device(
    vectors, reflectors, factors, tiles, tile_left, tile_right, tile_occupied_mask, channels
):
    count = lax.axis_size("row")
    vectors = pltpu.with_memory_space_constraint(vectors, pltpu.HBM)
    reflectors = pltpu.with_memory_space_constraint(reflectors, pltpu.HBM)
    want = passed_along(tile_right[0], "sym", 1)
    far = count // NEAR
    inside = [[far_at * NEAR + at for at in range(NEAR)] for far_at in range(far)]
    shares = local_grams(vectors, reflectors, NEAR).astype(F16)
    want, shares = lax.optimization_barrier((want, shares))
    terms = exchanged(shares, inside)
    owned = jnp.concatenate(combined([terms[at] for at in range(NEAR)]), axis=0)
    owned = owned.astype(F16)
    want, owned = lax.optimization_barrier((want, owned))
    named = fetched_blocks(want, vectors, reflectors)
    others = [around(owned, NEAR * step) for step in (1, far - 1, *range(2, far - 1))]
    others, named = lax.optimization_barrier((others, named))
    body, exponent = combined([owned, *others])
    copies = jnp.broadcast_to(body.astype(F16), (NEAR, BODY, 128))
    sums = exchanged(copies, inside).astype(F32)
    packed, upper, lower = solve_and_update(
        want, channels[0], sums, exponent, factors, *named
    )
    right = passed_along(packed, "sym", -1)
    left = left_products(
        tile_left[0],
        tile_occupied_mask[0],
        channels[0],
        upper,
        lower,
        vectors,
        reflectors,
        tiles,
    )
    partial = tile_products(*left, right)
    eigen = partial.shape[1]
    owned = exchanged(partial.reshape(count, eigen // count, eigen))
    return jnp.sum(owned.astype(F32), axis=0)[None]


def solution(mesh):
    return jax.shard_map(
        on_device,
        mesh=mesh,
        in_specs=(
            P("sym", "row", None),
            P("sym", "row", None),
            P("sym", None, None, None),
            P("sym", "row", None, None),
            P("sym", "row"),
            P("sym", "row"),
            P("sym", "row"),
            P("sym", "row"),
        ),
        out_specs=P("sym", "row", None),
        check_vma=False,
    )
```
